32 devices in a mesh: head: 2 (over x), ctx: 16 (over z, y, core).
Axes of the slice: x: 2, y: 2, z: 4, core: 2. Of those that a mesh axis runs over, the one named last changes fastest.
Arguments:
- queries: bfloat16 [8192, 32, 128], P('ctx', 'head'), may hold values from -1.75 to 1.75
- keys: bfloat16 [8192, 32, 128], P('ctx', 'head'), may hold values from -1.75 to 1.75
- values: bfloat16 [8192, 32, 128], P('ctx', 'head'), may hold values from -6 to 6
- out_grad: bfloat16 [8192, 32, 128], P('ctx', 'head'), may hold values from -6 to 6
- gain: float32 [32, 128], P('head'), may hold values from 0.25 to 1.75
- decay_rate: float32 [32], P('head'), may hold values from 1e-05 to 0.03
- doc_lengths: int32 [32], replicated, may hold values from 1 to 4096, 8192 in all
Outputs:
- q_grad: bfloat16 [8192, 32, 128], P('ctx', 'head')
- k_grad: bfloat16 [8192, 32, 128], P('ctx', 'head')
- v_grad: bfloat16 [8192, 32, 128], P('ctx', 'head')
The draws below stay inside these ranges and needn't reach their ends.
Inputs may be any that keep to these rules, and one draw needn't show every extreme that they name: `doc_lengths`: the lengths sum to 8192 and the longest is exactly 4096.
All inputs are finite; a program needn't handle non-finite values.
Results may differ from the reference program's by a relative error of at most 0.006.
Values sent between devices are 32-bit elements; how exact they have to be, the bound alone decides.
No kernel may reach another device: no remote copies, remote signals or barrier semaphores. Data moves between devices by JAX's collectives and lax.ppermute only.
A program may use at most 128 MiB of HBM per device.

```python
import math
from functools import partial
import jax
import jax.numpy as jnp
import numpy as np
from jax import lax

HEADS = 32
HEAD_DIM = 128
TOK_DEV = 512
TOKENS = 8192
NDOCS = 32
MOST = 4096


def draw_decay_rate(key, part):
    pick_key, slow_key, fast_key = jax.random.split(key, 3)
    share = 0.5
    slow_heads = jax.random.uniform(pick_key, (HEADS,), jnp.float32) < share
    slow_rates = jnp.exp(jax.random.uniform(slow_key, (HEADS,), jnp.float32, jnp.log(1e-05), jnp.log(0.0002)))
    fast_rates = jnp.exp(jax.random.uniform(fast_key, (HEADS,), jnp.float32, jnp.log(0.002), jnp.log(0.03)))
    return jnp.where(slow_heads, slow_rates, fast_rates).astype(jnp.float32)


def block_levels(key, extent, cuts, smallest, largest):
    level = 1.0
    for axis_at, parts in cuts:
        heights = jax.random.uniform(jax.random.fold_in(jax.random.fold_in(key, 6), axis_at), (parts,), jnp.float32, smallest / len(cuts), largest / len(cuts))
        level = level * jnp.repeat(jnp.exp(heights), extent[axis_at] // parts).reshape((-1,) + (1,) * (len(extent) - 1 - axis_at))
    return level


def profile(count, total, bound, skew):
    weights = [(1 << 20) // math.isqrt(rank ** skew) + 1 for rank in range(2, count + 1)]
    spare, given = total - bound - (count - 1), [1] * (count - 1)
    while spare > 0:
        free = [i for i in range(count - 1) if given[i] < bound]
        pool, remaining = sum([weights[i] for i in free]), spare
        for i in free:
            addition = min(bound - given[i], max(1, remaining * weights[i] // pool), spare)
            given[i] = given[i] + addition
            spare = spare - addition
    return np.array([bound] + given)


def ragged(own_key, amount, total, limit, skew):
    if amount == 2:
        one = jax.random.randint(own_key, (), max(1, total - limit), min(limit, total - 1) + 1)
        return jnp.stack([one, total - one])
    sizes = jnp.asarray(profile(amount, total, limit, skew), jnp.int32)
    couples = (amount - 1) // 2
    giver, receiver = sizes[1:1 + 2 * couples:2], sizes[2:2 + 2 * couples:2]
    margin = jnp.minimum(giver - 1, limit - receiver)
    shifted = jax.random.randint(jax.random.fold_in(own_key, 1), (couples,), 0, 1 << 20) % (margin + 1)
    sizes = sizes.at[1:1 + 2 * couples:2].set(giver - shifted).at[2:2 + 2 * couples:2].set(receiver + shifted)
    return sizes[jax.random.permutation(jax.random.fold_in(own_key, 2), amount)]


def centred(stream_key, dims, width, most, cuts=(), kind=jnp.bfloat16):
    result = width * jax.random.normal(stream_key, dims, jnp.float32)
    if cuts:
        result = result * block_levels(stream_key, dims, cuts, -0.22, 0.18)
    return jnp.clip(result, -most, most).astype(kind)


def setup_inputs(seed: int = 0) -> dict:
    streams_of = jax.random.split(jax.random.key(seed), 8)
    return {
        "queries": centred(streams_of[0], (TOKENS, HEADS, HEAD_DIM), 0.3, 1.75, ((0, 16), (1, 2))),
        "keys": centred(streams_of[1], (TOKENS, HEADS, HEAD_DIM), 0.3, 1.75, ((0, 16), (1, 2))),
        "values": centred(streams_of[2], (TOKENS, HEADS, HEAD_DIM), 1.0, 6.0, ((0, 16), (1, 2))),
        "out_grad": centred(streams_of[3], (TOKENS, HEADS, HEAD_DIM), 1.0, 6.0, ((0, 16), (1, 2))),
        "gain": jnp.clip(1.0 + 0.15 * jax.random.normal(streams_of[4], (HEADS, HEAD_DIM), jnp.float32), 0.25, 1.75),
        "decay_rate": draw_decay_rate(jax.random.fold_in(streams_of[7], 71), 0),
        "doc_lengths": ragged(streams_of[6], NDOCS, TOKENS, MOST, 2).astype(jnp.int32),
    }


epsilon = 1e-06

def mix(form, left, right):
    return jnp.einsum(form, left.astype(jnp.float32), right.astype(jnp.float32), preferred_element_type=jnp.float32, precision=lax.Precision.HIGHEST)

def decay_mask(segment, decays):
    block_len = segment.shape[0]
    offsets = jnp.arange(block_len, dtype=jnp.int32)
    distance = offsets[:, None] - offsets[None, :]
    allowed = (distance >= 0) & (segment[:, None] == segment[None, :])
    weight = jnp.exp(-decays[:, None, None] * jnp.maximum(distance, 0).astype(jnp.float32)[None])
    return jnp.where(allowed[None], weight, jnp.float32(0.0))

def forward_block(decays, carry, block):
    carried, prev_seg = carry
    queries_blk, key_blk, values_blk, segment = block
    block_len = segment.shape[0]
    offsets = jnp.arange(block_len, dtype=jnp.float32)
    weight = decay_mask(segment, decays)
    scores = mix('thd,shd->hts', queries_blk, key_blk)
    weighted = (scores * weight).astype(jnp.bfloat16)
    output = mix('hts,shd->thd', weighted, values_blk)
    in_factor = jnp.where((segment == prev_seg)[:, None], jnp.exp(-decays[None, :] * (offsets[:, None] + 1.0)), jnp.float32(0.0))
    output = output + in_factor[:, :, None] * mix('thd,hde->the', queries_blk, carried.astype(jnp.bfloat16))
    last_seg = segment[-1]
    tail = jnp.where((segment == last_seg)[:, None], jnp.exp(-decays[None, :] * (block_len - 1.0 - offsets)[:, None]), jnp.float32(0.0))
    own_part = mix('shd,she->hde', (key_blk * tail[:, :, None]).astype(jnp.bfloat16), values_blk)
    keep_factor = jnp.where(prev_seg == last_seg, jnp.exp(-decays * block_len), jnp.float32(0.0))
    return ((keep_factor[:, None, None] * carried + own_part, last_seg), (output, carried))

def gradient_block(decays, block):
    queries_blk, key_blk, values_blk, grad_blk, segment, carried, prev_seg = block
    block_len = segment.shape[0]
    offsets = jnp.arange(block_len, dtype=jnp.float32)
    weight = decay_mask(segment, decays)
    scores = mix('thd,shd->hts', queries_blk, key_blk)
    weighted = (scores * weight).astype(jnp.bfloat16)
    grad_scores = mix('thd,shd->hts', grad_blk, values_blk)
    grad_weights = (grad_scores * weight).astype(jnp.bfloat16)
    q_part = mix('hts,shd->thd', grad_weights, key_blk)
    k_part = mix('hts,thd->shd', grad_weights, queries_blk)
    v_part = mix('hts,thd->shd', weighted, grad_blk)
    in_factor = jnp.where((segment == prev_seg)[:, None], jnp.exp(-decays[None, :] * (offsets[:, None] + 1.0)), jnp.float32(0.0))
    q_part = q_part + in_factor[:, :, None] * mix('the,hde->thd', grad_blk, carried.astype(jnp.bfloat16))
    return (q_part, k_part, v_part)

def reverse_block(decays, carry, block):
    carried, next_seg = carry
    queries_blk, key_blk, values_blk, grad_blk, segment = block
    block_len = segment.shape[0]
    offsets = jnp.arange(block_len, dtype=jnp.float32)
    in_factor = jnp.where((segment == next_seg)[:, None], jnp.exp(-decays[None, :] * (block_len - offsets[:, None])), jnp.float32(0.0))
    packed = carried.astype(jnp.bfloat16)
    k_extra = in_factor[:, :, None] * mix('she,hde->shd', values_blk, packed)
    v_extra = in_factor[:, :, None] * mix('shd,hde->she', key_blk, packed)
    first_seg = segment[0]
    lead = jnp.where((segment == first_seg)[:, None], jnp.exp(-decays[None, :] * offsets[:, None]), jnp.float32(0.0))
    own_part = mix('thd,the->hde', (queries_blk * lead[:, :, None]).astype(jnp.bfloat16), grad_blk)
    keep_factor = jnp.where(first_seg == next_seg, jnp.exp(-decays * block_len), jnp.float32(0.0))
    return ((keep_factor[:, None, None] * carried + own_part, first_seg), (k_extra, v_extra))

def in_blocks(array, blocks):
    return array.reshape((blocks, array.shape[0] // blocks) + array.shape[1:])

def reference(queries, keys, values, out_grad, gain, decay_rate, doc_lengths):
    tok_total, head_count, head_dim = queries.shape
    block_len = min(512, TOK_DEV)
    blocks = tok_total // block_len
    starts = (jnp.cumsum(doc_lengths) - doc_lengths).astype(jnp.int32)
    start_flags = jnp.zeros((tok_total,), jnp.int32).at[starts].add(1)
    segment = (jnp.cumsum(start_flags) - 1).astype(jnp.int32)
    query_b = in_blocks(queries, blocks)
    key_b = in_blocks(keys, blocks)
    value_b = in_blocks(values, blocks)
    seg_b = in_blocks(segment, blocks)
    zero_state = jnp.zeros((head_count, head_dim, head_dim), jnp.float32)
    final_carry, (outs, entry_states) = lax.scan(partial(forward_block, decay_rate), (zero_state, jnp.array(-1, jnp.int32)), (query_b, key_b, value_b, seg_b))
    attn_out = outs.reshape(tok_total, head_count, head_dim)
    gained = gain[None] * out_grad.astype(jnp.float32)
    squares = lax.optimization_barrier(jnp.sum(attn_out * attn_out, axis=(1, 2)))
    cross = lax.optimization_barrier(jnp.sum(gained * attn_out, axis=(1, 2)))
    norm_width = head_count * head_dim
    inverse = 1.0 / jnp.sqrt(squares / norm_width + epsilon)
    grad_o = (gained * inverse[:, None, None] - attn_out * (cross * inverse * inverse * inverse / norm_width)[:, None, None]).astype(jnp.bfloat16)
    grad_b = in_blocks(grad_o, blocks)
    prev_blocks = jnp.concatenate([jnp.array([-1], jnp.int32), seg_b[:-1, -1]]).astype(jnp.int32)
    q_part, k_part, v_part = lax.map(partial(gradient_block, decay_rate), (query_b, key_b, value_b, grad_b, seg_b, entry_states, prev_blocks))
    back_carry, (k_extra, v_extra) = lax.scan(partial(reverse_block, decay_rate), (zero_state, jnp.array(-2, jnp.int32)), (query_b, key_b, value_b, grad_b, seg_b), reverse=True)
    shape = (tok_total, head_count, head_dim)
    q_grad = q_part.reshape(shape)
    k_grad = (k_part + k_extra).reshape(shape)
    v_grad = (v_part + v_extra).reshape(shape)
    return (q_grad.astype(jnp.bfloat16), k_grad.astype(jnp.bfloat16), v_grad.astype(jnp.bfloat16))
```

```python
from functools import partial

import jax
import jax.numpy as jnp
from jax import lax
from jax.experimental import pallas as pl
from jax.experimental.pallas import tpu as pltpu
from jax.sharding import PartitionSpec as P

EPSILON = 1e-06
LONGEST = 4096
FAR = 1e30
F32 = jnp.float32
BF16 = jnp.bfloat16


def dot(left, right, dims):
    return lax.dot_general(left, right, (dims, ((), ())), preferred_element_type=F32)


NN = ((1,), (0,))
NT = ((1,), (1,))
TN = ((0,), (0,))


def column(tokens, width):
    return lax.broadcasted_iota(jnp.int32, (tokens, width), 0)


def put_halves(core, ref, h, mine, other):
    half = mine.shape[0]
    ref[h, pl.ds(pl.multiple_of(core * half, half), half), :] = mine.astype(ref.dtype)
    ref[h, pl.ds(pl.multiple_of((1 - core) * half, half), half), :] = other.astype(ref.dtype)


def split_halves(core, state, send_ref, keep_ref, h):
    half = state.shape[0] // 2
    low, high = state[:half], state[half:]
    keep_ref[h] = jnp.where(core == 0, low, high)
    send_ref[h] = jnp.where(core == 0, high, low)


def state_kernel(first, docs_ref, rate_ref, k_ref, v_ref, kh_ref, vh_ref, send_ref, keep_ref):
    tokens, heads, dim = k_ref.shape
    index = lax.axis_index("ctx")
    end = (index + 1) * tokens

    def scan(j, carry):
        start, last = carry
        last = jnp.where(start <= end - 1, start, last)
        return (start + docs_ref[j], last)

    _, last = lax.fori_loop(0, docs_ref.shape[0], scan, (jnp.int32(0), jnp.int32(0)))
    row = column(tokens, dim)
    distance = jnp.where(
        row + index * tokens >= last, (tokens - 1 - row).astype(F32), F32(FAR)
    )
    kh_ref[...] = jnp.swapaxes(k_ref[...], 0, 1)
    vh_ref[...] = jnp.swapaxes(v_ref[...], 0, 1)
    core = index & 1
    for h in range(heads):
        tail = jnp.exp(-rate_ref[first + h] * distance)
        faded = (kh_ref[h].astype(F32) * tail).astype(BF16)
        split_halves(core, dot(faded, vh_ref[h], TN), send_ref, keep_ref, h)


def scores_kernel(first, rows, rate_ref, q_ref, g_ref, kh_ref, vh_ref, dist_ref, qh_ref, gh_ref, out_ref, probs_ref):
    tokens, heads, dim = q_ref.shape
    qh_ref[...] = jnp.swapaxes(q_ref[...], 0, 1)
    gh_ref[...] = jnp.swapaxes(g_ref[...], 0, 1)

    def head(h, carry):
        rate = rate_ref[first + h]
        for low in range(0, tokens, rows):
            top = low + rows
            scores = dot(qh_ref[h, low:top, :], kh_ref[h, :top, :], NT)
            decay = jnp.exp(-rate * dist_ref[low:top, :top])
            probs = (scores * decay).astype(BF16)
            probs_ref[h, low:top, :top] = probs
            out_ref[h, low:top, :] = dot(probs, vh_ref[h, :top, :], NN).astype(BF16)
        return carry

    lax.fori_loop(0, heads, head, 0)


def attend_kernel(first, begin, final, info_ref, rate_ref, qh_ref, gh_ref, local_ref, gain_ref, mine_ref, other_ref, *refs):
    if not begin:
        sum_ref, refs = refs[0], refs[1:]
    attn_ref, state_ref, stats_ref = refs[:3]
    heads, tokens, dim = qh_ref.shape
    core = info_ref[0] & 1
    row = column(tokens, dim)
    distance = jnp.where(
        row + info_ref[1] < info_ref[2], (row + 1).astype(F32), F32(FAR)
    )
    if begin:
        squares = jnp.zeros((tokens, dim), F32)
        cross = jnp.zeros((tokens, dim), F32)
    else:
        squares, cross = sum_ref[0], sum_ref[1]
    for h in range(heads):
        put_halves(core, state_ref, h, mine_ref[h], other_ref[h])
        factor = jnp.exp(-rate_ref[first + h] * distance)
        attn = local_ref[h].astype(F32) + factor * dot(qh_ref[h], state_ref[h], NN)
        attn_ref[h] = attn.astype(BF16)
        squares += attn * attn
        cross += gain_ref[h : h + 1, :] * gh_ref[h].astype(F32) * attn
    if final:
        stats_ref[0:1, :] = jnp.sum(jnp.swapaxes(squares, 0, 1), axis=0, keepdims=True)
        stats_ref[1:2, :] = jnp.sum(jnp.swapaxes(cross, 0, 1), axis=0, keepdims=True)
    else:
        stats_ref[0] = squares
        stats_ref[1] = cross


def norm_kernel(first, width, parts, info_ref, rate_ref, *refs):
    stats_refs, refs = refs[:parts], refs[parts:]
    attn_ref, gh_ref, qh_ref, gain_ref, grad_ref, send_ref, keep_ref = refs
    heads, tokens, dim = qh_ref.shape
    core = info_ref[0] & 1
    stats = stats_refs[0][...]
    for ref in stats_refs[1:]:
        stats = stats + ref[...]
    squares, cross = stats[0:1, :], stats[1:2, :]
    inverse = 1.0 / jnp.sqrt(squares / width + EPSILON)
    scale = cross * inverse * inverse * inverse / width
    inverse = jnp.swapaxes(jnp.broadcast_to(inverse, (dim, tokens)), 0, 1)
    scale = jnp.swapaxes(jnp.broadcast_to(scale, (dim, tokens)), 0, 1)
    row = column(tokens, dim)
    distance = jnp.where(row + info_ref[1] < info_ref[3], row.astype(F32), F32(FAR))
    for h in range(heads):
        gained = gain_ref[h : h + 1, :] * gh_ref[h].astype(F32)
        grad = (gained * inverse - attn_ref[h].astype(F32) * scale).astype(BF16)
        grad_ref[h] = grad
        lead = jnp.exp(-rate_ref[first + h] * distance)
        faded = (qh_ref[h].astype(F32) * lead).astype(BF16)
        split_halves(core, dot(faded, grad, TN), send_ref, keep_ref, h)


def grads_kernel(first, rows, info_ref, rate_ref, grad_ref, qh_ref, kh_ref, vh_ref, probs_ref, dist_ref, state_ref, *refs):
    dq_ref, dk_ref, dv_ref, dqh_ref = refs[-4:]
    heads, tokens, dim = qh_ref.shape
    row = column(tokens, dim)
    distance = jnp.where(
        row + info_ref[1] < info_ref[2], (row + 1).astype(F32), F32(FAR)
    )

    def head(h, carry):
        rate = rate_ref[first + h]
        factor = jnp.exp(-rate * distance)
        dk = dv = None
        for low in range(tokens - rows, -1, -rows):
            top = low + rows
            grad = grad_ref[h, low:top, :]
            raw = dot(grad, vh_ref[h, :top, :], NT)
            weights = (raw * jnp.exp(-rate * dist_ref[low:top, :top])).astype(BF16)
            dq = dot(weights, kh_ref[h, :top, :], NN)
            dq += factor[low:top] * dot(grad, state_ref[h], NT)
            dqh_ref[h, low:top, :] = dq.astype(BF16)
            dk_new = dot(weights, qh_ref[h, low:top, :], TN)
            dv_new = dot(probs_ref[h, low:top, :top], grad, TN)
            if dk is not None:
                dk_new += dk[:top]
                dv_new += dv[:top]
            dk, dv = dk_new, dv_new
            dk_ref[h, low:top, :] = dk[low:top].astype(BF16)
            dv_ref[h, low:top, :] = dv[low:top].astype(BF16)
        return carry

    lax.fori_loop(0, heads, head, 0)
    dq_ref[...] = jnp.swapaxes(dqh_ref[...], 0, 1)


def finish_kernel(first, info_ref, rate_ref, kh_ref, vh_ref, dk_part_ref, dv_part_ref, mine_ref, other_ref, *refs):
    dk_ref, dv_ref, dkh_ref, dvh_ref, state_ref = refs[-5:]
    heads, tokens, dim = kh_ref.shape
    core = info_ref[0] & 1
    row = column(tokens, dim)
    distance = jnp.where(
        row + info_ref[1] >= info_ref[4], (tokens - row).astype(F32), F32(FAR)
    )
    for h in range(heads):
        put_halves(core, state_ref, h, mine_ref[h], other_ref[h])
        factor = jnp.exp(-rate_ref[first + h] * distance)
        dk = dk_part_ref[h].astype(F32) + factor * dot(vh_ref[h], state_ref[h], NT)
        dv = dv_part_ref[h].astype(F32) + factor * dot(kh_ref[h], state_ref[h], NN)
        dkh_ref[h] = dk.astype(BF16)
        dvh_ref[h] = dv.astype(BF16)
    dk_ref[...] = jnp.swapaxes(dkh_ref[...], 0, 1)
    dv_ref[...] = jnp.swapaxes(dvh_ref[...], 0, 1)


def send(block, axis, target):
    count = lax.axis_size(axis)
    route = [(i, target(i)) for i in range(count) if 0 <= target(i) < count]
    return lax.ppermute(block, axis, route)


def weight_table(index, tokens, starts, rates, rows, shift):
    xors, ands, adds, xors2, ands2, adds2 = (jnp.array(c, jnp.int32) for c in zip(*rows))
    begin = (((index ^ xors) & ands) + adds) * tokens
    end = (((index ^ xors2) & ands2) + adds2) * tokens
    seg = lambda p: jnp.sum((starts[None, :] <= (p - shift)[:, None]).astype(jnp.int32), axis=1)
    fade = jnp.exp(-rates[None, :] * jnp.abs(end - begin).astype(F32)[:, None])
    return jnp.where((seg(begin) == seg(end))[:, None], fade, F32(0.0))


def hop_count(tokens):
    return -(-LONGEST // (4 * tokens))


def forward_rows(hops):
    c, p = ~1, ~3
    rows = [
        (0, -1, 1, 0, c, 2),
        (1, -1, 1, 0, c, 2),
        (0, c, 2, 0, p, 4),
        (2, c, 2, 0, p, 4),
        (0, p, 0, 0, p, 2),
        (0, c, 0, 0, c, 1),
    ]
    return rows + [(0, p, -4 * hop, 0, p, 0) for hop in range(hops)]


def backward_rows(hops):
    c, p = ~1, ~3
    rows = [
        (0, -1, 0, 0, c, 0),
        (1, -1, 0, 0, c, 0),
        (0, c, 0, 0, p, 0),
        (2, c, 0, 0, p, 0),
        (0, p, 4, 0, p, 2),
        (0, c, 2, 0, c, 1),
    ]
    return rows + [(0, p, 4 + 4 * hop, 0, p, 4) for hop in range(hops)]


def entering_state(send_half, keep_half, table, index, forward, hops):
    core, side = index & 1, (index >> 1) & 1
    core_first = core == (0 if forward else 1)
    side_first = side == (0 if forward else 1)
    step = 4 if forward else -4
    w = [table[j][:, None, None] for j in range(table.shape[0])]
    quarter = keep_half.shape[1] // 2
    one, zero = F32(1.0), F32(0.0)
    pick = lambda block, at: jnp.where(at == 0, block[:, :quarter], block[:, quarter:])

    came_half = send(send_half, "ctx", lambda i: i ^ 1)
    chip = w[0] * keep_half + w[1] * came_half
    earlier_half = jnp.where(core_first, keep_half, came_half)

    keep_part, send_part = pick(chip, side), pick(chip, 1 - side)
    came_part = send(send_part, "ctx", lambda i: i ^ 2)
    moving = w[2] * keep_part + w[3] * came_part
    earlier_part = jnp.where(side_first, keep_part, came_part)

    total = None
    for hop in range(hops):
        moving = send(moving, "ctx", lambda i: i + step)
        total = moving if total is None else total + w[6 + hop] * moving

    later = w[4] * total + earlier_part
    own = jnp.where(side_first, total, later)
    came = send(jnp.where(side_first, later, total), "ctx", lambda i: i ^ 2)
    half = jnp.where(
        side == 0,
        jnp.concatenate([own, came], axis=1),
        jnp.concatenate([came, own], axis=1),
    )
    later_half = w[5] * half + earlier_half
    mine = jnp.where(core_first, half, later_half)
    other = send(jnp.where(core_first, later_half, half), "ctx", lambda i: i ^ 1)
    return mine, other


def head_sum_parts(stats):
    count = lax.axis_size("head")
    if count & (count - 1):
        return [stats] + [
            lax.ppermute(stats, "head", [(i, (i + d) % count) for i in range(count)])
            for d in range(1, count)
        ]
    parts, bit = [stats], 1
    while bit < count:
        stats = parts[0] if len(parts) == 1 else parts[0] + parts[1]
        parts = [stats, send(stats, "head", lambda i: i ^ bit)]
        bit *= 2
    return parts


SMEM = pl.BlockSpec(memory_space=pltpu.SMEM)


def whole(array):
    zeros = (0,) * array.ndim
    return pl.BlockSpec(array.shape, lambda i: zeros)


def run(kernel, name, args, specs, outs, out_specs=None, scratch=(), alias=None, cost=(0, 0)):
    specs = [whole(a) if s is None else s for a, s in zip(args, specs)]
    out_specs = [whole(o) if s is None else s for o, s in zip(outs, out_specs or [None] * len(outs))]
    return pl.pallas_call(
        kernel,
        out_shape=outs,
        grid=(1,),
        in_specs=specs,
        out_specs=out_specs,
        scratch_shapes=scratch,
        input_output_aliases=alias or {},
        name=name,
        cost_estimate=pl.CostEstimate(flops=cost[0], bytes_accessed=cost[1], transcendentals=0),
        compiler_params=pltpu.CompilerParams(vmem_limit_bytes=48 << 20),
    )(*args)


def local(queries, keys, values, out_grad, gain, rates, docs):
    tokens, heads, dim = queries.shape
    count = 8 if heads % 8 == 0 else heads
    chunks = range(heads // count)
    rows = tokens // 2
    hops = hop_count(tokens)
    width = heads * dim * lax.axis_size("head")
    index = lax.axis_index("ctx").astype(jnp.int32)
    base = index * tokens
    shape = lambda *s, t=BF16: jax.ShapeDtypeStruct(s, t)
    major = shape(count, tokens, dim)
    half = shape(count, dim // 2, dim, t=F32)
    token_block = lambda c: pl.BlockSpec((tokens, count, dim), lambda i: (0, c, 0))
    gain_block = lambda c: pl.BlockSpec((count, dim), lambda i: (c, 0))
    unit = count * tokens * dim

    kh, vh, sends, keeps = [], [], [], []
    for c in chunks:
        a, b, s, k = run(
            partial(state_kernel, c * count),
            f"state{c}",
            [docs, rates, keys, values],
            [SMEM, SMEM, token_block(c), token_block(c)],
            [major, major, half, half],
            cost=(2 * unit * dim, 8 * unit),
        )
        kh.append(a), vh.append(b), sends.append(s), keeps.append(k)

    order = jnp.arange(docs.shape[0], dtype=jnp.int32)
    starts = jnp.sum(jnp.where(order[None, :] < order[:, None], docs[None, :], 0), axis=1)
    inf = jnp.int32(1 << 30)
    limits = jnp.stack(
        [
            index,
            base,
            jnp.min(jnp.where(starts >= base, starts, inf)),
            jnp.min(jnp.where(starts > base, starts, inf)),
            jnp.max(jnp.where(starts <= base + tokens, starts, 0)),
        ]
    )
    spots = jnp.arange(tokens, dtype=jnp.int32)
    begins = jnp.max(
        jnp.where(starts[None, :] <= (base + spots)[:, None], starts[None, :], 0), axis=1
    )
    distance = jnp.where(
        (spots[None, :] <= spots[:, None]) & (base + spots[None, :] >= begins[:, None]),
        (spots[:, None] - spots[None, :]).astype(F32),
        F32(FAR),
    )
    ahead = weight_table(index, tokens, starts, rates, forward_rows(hops), 1)
    back = weight_table(index, tokens, starts, rates, backward_rows(hops), 0)
    part = lambda table, c: table[:, c * count : (c + 1) * count]

    qh, gh, local_out, probs = [], [], [], []
    for c in chunks:
        a, b, o, p = run(
            partial(scores_kernel, c * count, rows),
            f"scores{c}",
            [rates, queries, out_grad, kh[c], vh[c], distance],
            [SMEM, token_block(c), token_block(c), None, None, None],
            [major, major, major, shape(count, tokens, tokens)],
            cost=(4 * unit * tokens, 24 * unit),
        )
        qh.append(a), gh.append(b), local_out.append(o), probs.append(p)

    attn, states = [], []
    stats = None
    for c in chunks:
        mine, other = entering_state(sends[c], keeps[c], part(ahead, c), index, True, hops)
        begin, final = c == 0, c == chunks[-1]
        args = [limits, rates, qh[c], gh[c], local_out[c], gain, mine, other]
        specs = [SMEM, SMEM, None, None, None, gain_block(c), None, None]
        if not begin:
            args.append(stats), specs.append(None)
        a, s, stats = run(
            partial(attend_kernel, c * count, begin, final),
            f"attend{c}",
            args,
            specs,
            [major, shape(count, dim, dim), shape(2, tokens, t=F32) if final else shape(2, tokens, dim, t=F32)],
            cost=(2 * unit * dim, 12 * unit),
        )
        attn.append(a), states.append(s)
    parts = head_sum_parts(stats)

    grads, sends, keeps = [], [], []
    for c in chunks:
        g, s, k = run(
            partial(norm_kernel, c * count, width, len(parts)),
            f"norm{c}",
            [limits, rates, *parts, attn[c], gh[c], qh[c], gain],
            [SMEM, SMEM] + [None] * (len(parts) + 3) + [gain_block(c)],
            [major, half, half],
            cost=(2 * unit * dim, 8 * unit),
        )
        grads.append(g), sends.append(s), keeps.append(k)

    full = shape(tokens, heads, dim)
    dq, dk_part, dv_part = None, [], []
    for c in chunks:
        args = [limits, rates, grads[c], qh[c], kh[c], vh[c], probs[c], distance, states[c]]
        specs = [SMEM, SMEM] + [None] * 7
        alias = {}
        if dq is not None:
            alias = {len(args): 0}
            args.append(dq), specs.append(pl.BlockSpec(memory_space=pl.ANY))
        dq, a, b = run(
            partial(grads_kernel, c * count, rows),
            f"grads{c}",
            args,
            specs,
            [full, major, major],
            [token_block(c), None, None],
            scratch=[pltpu.VMEM((count, tokens, dim), BF16)],
            alias=alias,
            cost=(8 * unit * tokens, 32 * unit),
        )
        dk_part.append(a), dv_part.append(b)

    dk = dv = None
    for c in chunks:
        mine, other = entering_state(sends[c], keeps[c], part(back, c), index, False, hops)
        args = [limits, rates, kh[c], vh[c], dk_part[c], dv_part[c], mine, other]
        specs = [SMEM, SMEM] + [None] * 6
        alias = {}
        if dk is not None:
            alias = {len(args): 0, len(args) + 1: 1}
            args += [dk, dv]
            specs += [pl.BlockSpec(memory_space=pl.ANY)] * 2
        dk, dv = run(
            partial(finish_kernel, c * count),
            f"finish{c}",
            args,
            specs,
            [full, full],
            [token_block(c), token_block(c)],
            scratch=[pltpu.VMEM((count, tokens, dim), BF16)] * 2 + [pltpu.VMEM((count, dim, dim), BF16)],
            alias=alias,
            cost=(4 * unit * dim, 14 * unit),
        )
    return dq, dk, dv


def solution(mesh):
    token, head = P("ctx", "head", None), P("head")
    return jax.shard_map(
        local,
        mesh=mesh,
        in_specs=(token, token, token, token, P("head", None), head, P()),
        out_specs=(token, token, token),
        check_vma=False,
    )
```

```python
from functools import partial

import jax
import jax.numpy as jnp
from jax import lax
from jax.experimental import pallas as pl
from jax.experimental.pallas import tpu as pltpu
from jax.sharding import PartitionSpec as P


EPSILON = 1e-06
LONGEST = 4096
FAR = 1e30
APART = 1 << 30
F32 = jnp.float32
BF16 = jnp.bfloat16


def dot(left, right, dims):
    return lax.dot_general(left, right, (dims, ((), ())), preferred_element_type=F32)


NN = ((1,), (0,))
NT = ((1,), (1,))
TN = ((0,), (0,))


def column(tokens, width):
    return lax.broadcasted_iota(jnp.int32, (tokens, width), 0)


def put_halves(core, ref, h, mine, other):
    half = mine.shape[0]
    ref[h, pl.ds(pl.multiple_of(core * half, half), half), :] = mine.astype(ref.dtype)
    ref[h, pl.ds(pl.multiple_of((1 - core) * half, half), half), :] = other.astype(ref.dtype)


def split_halves(core, state, send_ref, keep_ref, h):
    half = state.shape[0] // 2
    low, high = state[:half], state[half:]
    keep_ref[h] = jnp.where(core == 0, low, high)
    send_ref[h] = jnp.where(core == 0, high, low)


INDEX, BASE, NEXT_START, LATER_START, NEXT_BEGIN, FADES = range(6)


def fade_rows(hops):
    c, p = ~1, ~3
    ahead = [
        (0, -1, 1, 0, c, 2),
        (1, -1, 1, 0, c, 2),
        (0, c, 2, 0, p, 4),
        (2, c, 2, 0, p, 4),
        (0, p, 0, 0, p, 2),
        (0, c, 0, 0, c, 1),
    ]
    back = [
        (0, -1, 0, 0, c, 0),
        (1, -1, 0, 0, c, 0),
        (0, c, 0, 0, p, 0),
        (2, c, 0, 0, p, 0),
        (0, p, 4, 0, p, 2),
        (0, c, 2, 0, c, 1),
    ]
    ahead += [(0, p, -4 * hop, 0, p, 0) for hop in range(1, hops)]
    back += [(0, p, 4 + 4 * hop, 0, p, 4) for hop in range(1, hops)]
    return ahead, back


def setup_kernel(hops, docs_ref, info_ref, dist_ref, begin_ref):
    tokens = dist_ref.shape[0]
    lanes = begin_ref.shape[1]
    index = lax.axis_index("ctx").astype(jnp.int32)
    base = index * tokens
    ahead, back = fade_rows(hops)
    spot = lambda x, a, d: (((index ^ x) & a) + d) * tokens
    spans = [(spot(*row[:3]), spot(*row[3:])) for row in ahead + back]
    tops = [end - 1 for _, end in spans[: len(ahead)]] + [begin for begin, _ in spans[len(ahead) :]]
    tops.append(base + tokens)
    row = column(tokens, lanes)
    begin_ref[...] = jnp.zeros_like(begin_ref)

    def doc(j, carry):
        start, upper, later, seen = carry
        upper = jnp.where((start >= base) & (start < upper), start, upper)
        later = jnp.where((start > base) & (start < later), start, later)
        seen = tuple(jnp.where(start <= top, start, old) for top, old in zip(tops, seen))

        @pl.when((start > base) & (start < base + tokens))
        def _():
            begin_ref[...] = jnp.where(row >= start - base, start - base, begin_ref[...])

        return start + docs_ref[j], upper, later, seen

    zero = jnp.int32(0)
    far = jnp.int32(APART)
    _, upper, later, seen = lax.fori_loop(
        0, docs_ref.shape[0], doc, (zero, far, far, (zero,) * len(tops))
    )
    info_ref[INDEX] = index
    info_ref[BASE] = base
    info_ref[NEXT_START] = upper
    info_ref[LATER_START] = later
    info_ref[NEXT_BEGIN] = seen[-1]
    for j, ((begin, end), last) in enumerate(zip(spans, seen)):
        forward = j < len(ahead)
        joined = last < begin if forward else last <= end
        info_ref[FADES + j] = jnp.where(joined, end - begin if forward else begin - end, far)

    for low in range(0, tokens, lanes):
        spots = low + lax.broadcasted_iota(jnp.int32, (tokens, lanes), 1)
        allowed = (spots <= row) & (spots >= begin_ref[...])
        dist_ref[:, low : low + lanes] = jnp.where(allowed, (row - spots).astype(F32), F32(FAR))


def fade(rate, distance, shape):
    return jnp.exp(jnp.full(shape, -rate * distance.astype(F32), F32))


def spread(factor, block):
    return (block.reshape(-1, *factor.shape) * factor[None]).reshape(block.shape)


TILE = (8, 128)


def chip_kernel(at, info_ref, rate_ref, keep_ref, came_ref, keep_part_ref, send_part_ref):
    heads, quarter, _ = keep_part_ref.shape
    side = (info_ref[INDEX] >> 1) & 1
    for h in range(heads):
        rate = rate_ref[h]
        mine = fade(rate, info_ref[at], TILE)
        theirs = fade(rate, info_ref[at + 1], TILE)
        chip = spread(mine, keep_ref[h]) + spread(theirs, came_ref[h])
        low, high = chip[:quarter], chip[quarter:]
        keep_part_ref[h] = jnp.where(side == 0, low, high)
        send_part_ref[h] = jnp.where(side == 0, high, low)


def plane_kernel(at, info_ref, rate_ref, keep_ref, came_ref, out_ref):
    for h in range(out_ref.shape[0]):
        rate = rate_ref[h]
        mine = fade(rate, info_ref[at + 2], TILE)
        theirs = fade(rate, info_ref[at + 3], TILE)
        out_ref[h] = spread(mine, keep_ref[h]) + spread(theirs, came_ref[h])


def part_kernel(at, hops, first_side, info_ref, rate_ref, keep_ref, came_ref, *refs):
    moved, (own_ref, send_ref) = refs[:hops], refs[hops:]
    is_first = ((info_ref[INDEX] >> 1) & 1) == first_side
    for h in range(own_ref.shape[0]):
        rate = rate_ref[h]
        total = moved[0][h]
        for hop in range(1, hops):
            total += spread(fade(rate, info_ref[at + 5 + hop], TILE), moved[hop][h])
        earlier = jnp.where(is_first, keep_ref[h], came_ref[h])
        later = spread(fade(rate, info_ref[at + 4], TILE), total) + earlier
        own_ref[h] = jnp.where(is_first, total, later)
        send_ref[h] = jnp.where(is_first, later, total)


def half_kernel(at, first_core, info_ref, rate_ref, keep_ref, came_ref, own_ref, came_part_ref, mine_ref, send_ref):
    heads = own_ref.shape[0]
    index = info_ref[INDEX]
    is_first = (index & 1) == first_core
    low_side = ((index >> 1) & 1) == 0
    for h in range(heads):
        own, came = own_ref[h], came_part_ref[h]
        half = jnp.concatenate(
            [jnp.where(low_side, own, came), jnp.where(low_side, came, own)], axis=0
        )
        earlier = jnp.where(is_first, keep_ref[h], came_ref[h])
        later = spread(fade(rate_ref[h], info_ref[at + 5], TILE), half) + earlier
        mine_ref[h] = jnp.where(is_first, half, later).astype(BF16)
        send_ref[h] = jnp.where(is_first, later, half)


def state_kernel(docs_ref, rate_ref, k_ref, v_ref, kh_ref, vh_ref, send_ref, keep_ref):
    tokens, heads, dim = k_ref.shape
    first = pl.program_id(0) * heads
    index = lax.axis_index("ctx")
    end = (index + 1) * tokens

    def scan(j, carry):
        start, last = carry
        last = jnp.where(start <= end - 1, start, last)
        return (start + docs_ref[j], last)

    _, last = lax.fori_loop(0, docs_ref.shape[0], scan, (jnp.int32(0), jnp.int32(0)))
    row = column(tokens, dim)
    distance = jnp.where(
        row + index * tokens >= last, (tokens - 1 - row).astype(F32), F32(FAR)
    )
    turned_k = jnp.swapaxes(k_ref[...], 0, 1)
    turned_v = jnp.swapaxes(v_ref[...], 0, 1)
    kh_ref[pl.ds(first, heads)] = turned_k
    vh_ref[pl.ds(first, heads)] = turned_v
    core = index & 1
    for h in range(heads):
        tail = jnp.exp(-rate_ref[first + h] * distance)
        faded = (turned_k[h].astype(F32) * tail).astype(BF16)
        split_halves(core, dot(faded, turned_v[h], TN), send_ref, keep_ref, h)


def turn_kernel(q_ref, g_ref, qh_ref, gh_ref):
    heads = q_ref.shape[1]
    here = pl.ds(pl.program_id(0) * heads, heads)
    qh_ref[here] = jnp.swapaxes(q_ref[...], 0, 1)
    gh_ref[here] = jnp.swapaxes(g_ref[...], 0, 1)


def scores_kernel(first, rows, rate_ref, qh_ref, kh_ref, vh_ref, dist_ref, out_ref, probs_ref):
    heads, tokens, _ = out_ref.shape

    def head(h, carry):
        full = first + h
        rate = rate_ref[full]
        for low in range(0, tokens, rows):
            top = low + rows
            scores = dot(qh_ref[full, low:top, :], kh_ref[full, :top, :], NT)
            decay = jnp.exp(-rate * dist_ref[low:top, :top])
            probs = (scores * decay).astype(BF16)
            probs_ref[h, low:top, :top] = probs
            out_ref[h, low:top, :] = dot(probs, vh_ref[full, :top, :], NN).astype(BF16)
        return carry

    lax.fori_loop(0, heads, head, 0)


def attend_kernel(groups, info_ref, rate_ref, qh_ref, gh_ref, gain_ref, mine_ref, other_ref, *refs):
    local_refs, (attn_ref, state_ref, stats_ref) = refs[:groups], refs[groups:]
    heads, tokens, dim = qh_ref.shape
    count = heads // groups
    core = info_ref[INDEX] & 1
    row = column(tokens, dim)
    distance = jnp.where(
        row + info_ref[BASE] < info_ref[NEXT_START], (row + 1).astype(F32), F32(FAR)
    )
    squares = jnp.zeros((tokens, dim), F32)
    cross = jnp.zeros((tokens, dim), F32)
    for h in range(heads):
        put_halves(core, state_ref, h, mine_ref[h], other_ref[h])
        factor = jnp.exp(-rate_ref[h] * distance)
        near = local_refs[h // count][h % count].astype(F32)
        attn = near + factor * dot(qh_ref[h], state_ref[h], NN)
        attn_ref[h] = attn.astype(BF16)
        squares += attn * attn
        cross += gain_ref[h : h + 1, :] * gh_ref[h].astype(F32) * attn
    stats_ref[0:1, :] = jnp.sum(jnp.swapaxes(squares, 0, 1), axis=0, keepdims=True)
    stats_ref[1:2, :] = jnp.sum(jnp.swapaxes(cross, 0, 1), axis=0, keepdims=True)


def norm_kernel(width, parts, info_ref, rate_ref, *refs):
    stats_refs, refs = refs[:parts], refs[parts:]
    attn_ref, gh_ref, qh_ref, gain_ref, grad_ref, send_ref, keep_ref = refs
    heads, tokens, dim = qh_ref.shape
    core = info_ref[INDEX] & 1
    stats = stats_refs[0][...]
    for ref in stats_refs[1:]:
        stats = stats + ref[...]
    squares, cross = stats[0:1, :], stats[1:2, :]
    inverse = 1.0 / jnp.sqrt(squares / width + EPSILON)
    scale = cross * inverse * inverse * inverse / width
    inverse = jnp.swapaxes(jnp.broadcast_to(inverse, (dim, tokens)), 0, 1)
    scale = jnp.swapaxes(jnp.broadcast_to(scale, (dim, tokens)), 0, 1)
    row = column(tokens, dim)
    distance = jnp.where(row + info_ref[BASE] < info_ref[LATER_START], row.astype(F32), F32(FAR))
    for h in range(heads):
        gained = gain_ref[h : h + 1, :] * gh_ref[h].astype(F32)
        grad = (gained * inverse - attn_ref[h].astype(F32) * scale).astype(BF16)
        grad_ref[h] = grad
        lead = jnp.exp(-rate_ref[h] * distance)
        faded = (qh_ref[h].astype(F32) * lead).astype(BF16)
        split_halves(core, dot(faded, grad, TN), send_ref, keep_ref, h)


def grads_kernel(first, rows, info_ref, rate_ref, grad_ref, qh_ref, kh_ref, vh_ref, probs_ref, dist_ref, state_ref, dq_ref, dk_ref, dv_ref):
    heads, tokens, dim = dq_ref.shape
    row = column(tokens, dim)
    distance = jnp.where(
        row + info_ref[BASE] < info_ref[NEXT_START], (row + 1).astype(F32), F32(FAR)
    )

    def head(h, carry):
        full = first + h
        rate = rate_ref[full]
        factor = jnp.exp(-rate * distance)
        dk = dv = None
        for low in range(tokens - rows, -1, -rows):
            top = low + rows
            grad = grad_ref[full, low:top, :]
            raw = dot(grad, vh_ref[full, :top, :], NT)
            weights = (raw * jnp.exp(-rate * dist_ref[low:top, :top])).astype(BF16)
            dq = dot(weights, kh_ref[full, :top, :], NN)
            dq += factor[low:top] * dot(grad, state_ref[full], NT)
            dq_ref[h, low:top, :] = dq.astype(BF16)
            dk_new = dot(weights, qh_ref[full, low:top, :], TN)
            dv_new = dot(probs_ref[h, low:top, :top], grad, TN)
            if dk is not None:
                dk_new += dk[:top]
                dv_new += dv[:top]
            dk, dv = dk_new, dv_new
            dk_ref[h, low:top, :] = dk[low:top].astype(BF16)
            dv_ref[h, low:top, :] = dv[low:top].astype(BF16)
        return carry

    lax.fori_loop(0, heads, head, 0)


def turn_back_kernel(steps, *refs):
    parts, out_ref = refs[:-1], refs[-1]
    each = len(parts) // steps
    for s in range(steps):

        @pl.when(pl.program_id(0) == s)
        def _():
            block = [ref[...] for ref in parts[s * each : (s + 1) * each]]
            out_ref[...] = jnp.swapaxes(jnp.concatenate(block, axis=0), 0, 1)


def finish_kernel(groups, info_ref, rate_ref, kh_ref, vh_ref, mine_ref, other_ref, *refs):
    dk_parts, dv_parts = refs[:groups], refs[groups : 2 * groups]
    dk_ref, dv_ref, dkh_ref, dvh_ref, state_ref = refs[2 * groups :]
    heads, tokens, dim = dkh_ref.shape
    count = dk_parts[0].shape[0]
    core = info_ref[INDEX] & 1
    row = column(tokens, dim)
    distance = jnp.where(
        row + info_ref[BASE] >= info_ref[NEXT_BEGIN], (tokens - row).astype(F32), F32(FAR)
    )
    for s in range(groups * count // heads):

        @pl.when(pl.program_id(0) == s)
        def _():
            for h in range(heads):
                full = s * heads + h
                put_halves(core, state_ref, h, mine_ref[h], other_ref[h])
                factor = jnp.exp(-rate_ref[full] * distance)
                dk = dk_parts[full // count][full % count].astype(F32)
                dv = dv_parts[full // count][full % count].astype(F32)
                dk += factor * dot(vh_ref[full], state_ref[h], NT)
                dv += factor * dot(kh_ref[full], state_ref[h], NN)
                dkh_ref[h] = dk.astype(BF16)
                dvh_ref[h] = dv.astype(BF16)
            dk_ref[...] = jnp.swapaxes(dkh_ref[...], 0, 1)
            dv_ref[...] = jnp.swapaxes(dvh_ref[...], 0, 1)


def send(block, axis, target):
    count = lax.axis_size(axis)
    route = [(i, target(i)) for i in range(count) if 0 <= target(i) < count]
    return lax.ppermute(block, axis, route)


def hop_count(tokens):
    return -(-LONGEST // (4 * tokens))


def entering_state(leave, keep, info, rates, forward, hops):
    heads, rows, dim = keep.shape
    at = FADES + (0 if forward else len(fade_rows(hops)[0]))
    first = 0 if forward else 1
    step = 4 if forward else -4
    part = jax.ShapeDtypeStruct((heads, rows // 2, dim), F32)
    half = jax.ShapeDtypeStruct(keep.shape, F32)

    def combine(kernel, arrays, outs):
        return run(
            kernel,
            [info, rates, *arrays],
            [SMEM, SMEM] + [VMEM] * len(arrays),
            outs,
            [VMEM] * len(outs),
            cost=(0, 4 * heads * rows * dim),
        )

    came_half = send(leave, "ctx", lambda i: i ^ 1)
    keep_part, send_part = combine(partial(chip_kernel, at), [keep, came_half], [part] * 2)
    came_part = send(send_part, "ctx", lambda i: i ^ 2)
    (moving,) = combine(partial(plane_kernel, at), [keep_part, came_part], [part])
    moved = []
    for _ in range(hops):
        moving = send(moving, "ctx", lambda i: i + step)
        moved.append(moving)
    own, send_part = combine(
        partial(part_kernel, at, hops, first), [keep_part, came_part, *moved], [part] * 2
    )
    came = send(send_part, "ctx", lambda i: i ^ 2)
    mine, send_half = combine(
        partial(half_kernel, at, first),
        [keep, came_half, own, came],
        [jax.ShapeDtypeStruct(keep.shape, BF16), half],
    )
    return mine, send(send_half, "ctx", lambda i: i ^ 1)


def head_sum_parts(stats):
    count = lax.axis_size("head")
    if count & (count - 1):
        return [stats] + [
            lax.ppermute(stats, "head", [(i, (i + d) % count) for i in range(count)])
            for d in range(1, count)
        ]
    parts, bit = [stats], 1
    while bit < count:
        stats = parts[0] if len(parts) == 1 else parts[0] + parts[1]
        parts = [stats, send(stats, "head", lambda i: i ^ bit)]
        bit *= 2
    return parts


SMEM = pl.BlockSpec(memory_space=pltpu.SMEM)
VMEM = pl.BlockSpec(memory_space=pltpu.VMEM)


def kept(*arrays):
    return [pltpu.with_memory_space_constraint(a, pltpu.VMEM) for a in arrays]


def streamed(*arrays):
    return [pltpu.with_memory_space_constraint(a, pltpu.HBM) for a in arrays]


def run(kernel, args, specs, outs, out_specs, steps=None, scratch=(), cost=(0, 0)):
    return pl.pallas_call(
        kernel,
        out_shape=outs,
        grid=() if steps is None else (steps,),
        in_specs=specs,
        out_specs=out_specs,
        scratch_shapes=scratch,
        cost_estimate=pl.CostEstimate(flops=cost[0], bytes_accessed=cost[1], transcendentals=0),
        compiler_params=pltpu.CompilerParams(vmem_limit_bytes=16 << 20),
    )(*args)


def body(queries, keys, values, out_grad, gain, rates, docs):
    tokens, heads, dim = queries.shape
    wide = 8 if heads % 8 == 0 else heads
    count = 4 if heads % 4 == 0 else heads
    groups, steps = heads // count, heads // wide
    rows = tokens // 2
    hops = hop_count(tokens)
    width = heads * dim * lax.axis_size("head")
    shape = lambda *s: jax.ShapeDtypeStruct(s, F32)
    major = pltpu.VMEM((heads, tokens, dim), BF16)
    some = pltpu.VMEM((count, tokens, dim), BF16)
    half = shape(heads, dim // 2, dim)
    token_block = pl.BlockSpec((tokens, wide, dim), lambda i: (0, i, 0))
    half_block = pl.BlockSpec((wide, dim // 2, dim), lambda i: (i, 0, 0))
    unit = heads * tokens * dim

    kh, vh, leave, keep = run(
        state_kernel,
        [docs, rates, *streamed(keys, values)],
        [SMEM, SMEM, token_block, token_block],
        [major, major, half, half],
        [VMEM, VMEM, half_block, half_block],
        steps=steps,
        cost=(2 * unit * dim, 8 * unit),
    )

    spans = sum(len(rows) for rows in fade_rows(hops))
    limits, distance = run(
        partial(setup_kernel, hops),
        [docs],
        [SMEM],
        [jax.ShapeDtypeStruct((FADES + spans,), jnp.int32), pltpu.VMEM((tokens, tokens), F32)],
        [SMEM, VMEM],
        scratch=[pltpu.VMEM((tokens, dim), jnp.int32)],
        cost=(0, 2 * tokens * tokens),
    )

    qh, gh = run(
        turn_kernel,
        streamed(queries, out_grad),
        [token_block, token_block],
        [major, major],
        [VMEM, VMEM],
        steps=steps,
        cost=(0, 8 * unit),
    )
    near, probs = [], []
    for g in range(groups):
        n, p = run(
            partial(scores_kernel, g * count, rows),
            [rates, *kept(qh, kh, vh, distance)],
            [SMEM] + [VMEM] * 4,
            [some, pltpu.VMEM((count, tokens, tokens), BF16)],
            [VMEM] * 2,
            cost=(4 * unit * tokens // groups, 0),
        )
        near.append(n), probs.append(p)

    mine, other = entering_state(leave, keep, limits, rates, True, hops)
    attn, states, stats = run(
        partial(attend_kernel, groups),
        [limits, rates, *kept(qh, gh), gain, mine, other, *kept(*near)],
        [SMEM, SMEM] + [VMEM] * (5 + groups),
        [major, pltpu.VMEM((heads, dim, dim), BF16), shape(2, tokens)],
        [VMEM] * 3,
        cost=(2 * unit * dim, 4 * unit),
    )
    parts = head_sum_parts(stats)

    grads, leave, keep = run(
        partial(norm_kernel, width, len(parts)),
        [limits, rates, *parts, *kept(attn, gh, qh), gain],
        [SMEM, SMEM] + [VMEM] * (len(parts) + 4),
        [major, half, half],
        [VMEM] * 3,
        cost=(2 * unit * dim, 4 * unit),
    )

    dqh, dk_part, dv_part = [], [], []
    for g in range(groups):
        a, b, c = run(
            partial(grads_kernel, g * count, rows),
            [limits, rates, *kept(grads, qh, kh, vh, probs[g], distance, states)],
            [SMEM, SMEM] + [VMEM] * 7,
            [some] * 3,
            [VMEM] * 3,
            cost=(8 * unit * tokens // groups, 0),
        )
        dqh.append(a), dk_part.append(b), dv_part.append(c)
    full = jax.ShapeDtypeStruct((tokens, heads, dim), BF16)
    dq = run(
        partial(turn_back_kernel, steps),
        kept(*dqh),
        [VMEM] * groups,
        full,
        token_block,
        steps=steps,
        cost=(0, 2 * unit),
    )

    mine, other = entering_state(leave, keep, limits, rates, False, hops)
    dk, dv = run(
        partial(finish_kernel, groups),
        [limits, rates, *kept(kh, vh), mine, other, *kept(*dk_part, *dv_part)],
        [SMEM, SMEM, VMEM, VMEM, half_block, half_block] + [VMEM] * (2 * groups),
        [full, full],
        [token_block, token_block],
        steps=steps,
        scratch=[pltpu.VMEM((wide, tokens, dim), BF16)] * 2 + [pltpu.VMEM((wide, dim, dim), BF16)],
        cost=(4 * unit * dim, 4 * unit),
    )
    return dq, dk, dv


def solution(mesh):
    token, head = P("ctx", "head", None), P("head")
    return jax.shard_map(
        body,
        mesh=mesh,
        in_specs=(token, token, token, token, P("head", None), head, P()),
        out_specs=(token, token, token),
        check_vma=False,
    )
```

```python
from functools import partial

import jax
import jax.numpy as jnp
from jax import lax
from jax.experimental import pallas as pl
from jax.experimental.pallas import tpu as pltpu
from jax.sharding import PartitionSpec as P


EPSILON = 1e-06
LONGEST = 4096
FAR = 1e30
APART = 1 << 30
CHUNKS = 1
F32 = jnp.float32
BF16 = jnp.bfloat16


def dot(left, right, dims):
    return lax.dot_general(left, right, (dims, ((), ())), preferred_element_type=F32)


NN = ((1,), (0,))
NT = ((1,), (1,))
TN = ((0,), (0,))


def column(tokens, width):
    return lax.broadcasted_iota(jnp.int32, (tokens, width), 0)


def put_halves(core, ref, h, mine, other):
    half = mine.shape[0]
    ref[h, pl.ds(pl.multiple_of(core * half, half), half), :] = mine.astype(ref.dtype)
    ref[h, pl.ds(pl.multiple_of((1 - core) * half, half), half), :] = other.astype(ref.dtype)


def split_halves(core, state, send_ref, keep_ref, h):
    half = state.shape[0] // 2
    low, high = state[:half], state[half:]
    keep_ref[h] = jnp.where(core == 0, low, high)
    send_ref[h] = jnp.where(core == 0, high, low)


INDEX, BASE, NEXT_START, LATER_START, NEXT_BEGIN, FADES = range(6)


def fade_rows(hops):
    c, p = ~1, ~3
    ahead = [
        (0, -1, 1, 0, c, 2),
        (1, -1, 1, 0, c, 2),
        (0, c, 2, 0, p, 4),
        (2, c, 2, 0, p, 4),
        (0, p, 0, 0, p, 2),
        (0, c, 0, 0, c, 1),
    ]
    back = [
        (0, -1, 0, 0, c, 0),
        (1, -1, 0, 0, c, 0),
        (0, c, 0, 0, p, 0),
        (2, c, 0, 0, p, 0),
        (0, p, 4, 0, p, 2),
        (0, c, 2, 0, c, 1),
    ]
    ahead += [(0, p, -4 * hop, 0, p, 0) for hop in range(1, hops)]
    back += [(0, p, 4 + 4 * hop, 0, p, 4) for hop in range(1, hops)]
    return ahead, back


def setup_kernel(hops, tokens, docs_ref, rate_in_ref, info_ref, rate_ref):
    for h in range(rate_ref.shape[0]):
        rate_ref[h] = rate_in_ref[h]
    index = lax.axis_index("ctx").astype(jnp.int32)
    base = index * tokens
    ahead, back = fade_rows(hops)
    spot = lambda x, a, d: (((index ^ x) & a) + d) * tokens
    spans = [(spot(*row[:3]), spot(*row[3:])) for row in ahead + back]
    tops = [end - 1 for _, end in spans[: len(ahead)]] + [begin for begin, _ in spans[len(ahead) :]]
    tops.append(base + tokens)

    def doc(j, carry):
        start, upper, later, seen = carry
        upper = jnp.where((start >= base) & (start < upper), start, upper)
        later = jnp.where((start > base) & (start < later), start, later)
        seen = tuple(jnp.where(start <= top, start, old) for top, old in zip(tops, seen))
        return start + docs_ref[j], upper, later, seen

    zero = jnp.int32(0)
    far = jnp.int32(APART)
    _, upper, later, seen = lax.fori_loop(
        0, docs_ref.shape[0], doc, (zero, far, far, (zero,) * len(tops))
    )
    info_ref[INDEX] = index
    info_ref[BASE] = base
    info_ref[NEXT_START] = upper
    info_ref[LATER_START] = later
    info_ref[NEXT_BEGIN] = seen[-1]
    for j, ((begin, end), last) in enumerate(zip(spans, seen)):
        forward = j < len(ahead)
        joined = last < begin if forward else last <= end
        info_ref[FADES + j] = jnp.where(joined, end - begin if forward else begin - end, far)


def mask_kernel(docs_ref, dist_ref, begin_ref):
    tokens, lanes = begin_ref.shape
    base = lax.axis_index("ctx").astype(jnp.int32) * tokens
    row = column(tokens, lanes)
    begin_ref[...] = jnp.zeros_like(begin_ref)

    def doc(j, start):
        @pl.when((start > base) & (start < base + tokens))
        def _():
            begin_ref[...] = jnp.where(row >= start - base, start - base, begin_ref[...])

        return start + docs_ref[j]

    lax.fori_loop(0, docs_ref.shape[0], doc, jnp.int32(0))
    for low in range(0, tokens, lanes):
        spots = low + lax.broadcasted_iota(jnp.int32, (tokens, lanes), 1)
        allowed = (spots <= row) & (spots >= begin_ref[...])
        dist_ref[:, low : low + lanes] = jnp.where(allowed, (row - spots).astype(F32), F32(FAR))


def fade(rate, distance, shape):
    return jnp.exp(jnp.full(shape, -rate * distance.astype(F32), F32))


def spread(factor, block):
    return (block.reshape(-1, *factor.shape) * factor[None]).reshape(block.shape)


TILE = (8, 128)


def chip_kernel(at, base, info_ref, rate_ref, keep_ref, came_ref, keep_part_ref, send_part_ref):
    heads, quarter, _ = keep_part_ref.shape
    side = (info_ref[INDEX] >> 1) & 1
    for h in range(heads):
        rate = rate_ref[base + h]
        mine = fade(rate, info_ref[at], TILE)
        theirs = fade(rate, info_ref[at + 1], TILE)
        chip = spread(mine, keep_ref[h]) + spread(theirs, came_ref[h])
        low, high = chip[:quarter], chip[quarter:]
        keep_part_ref[h] = jnp.where(side == 0, low, high)
        send_part_ref[h] = jnp.where(side == 0, high, low)


def plane_kernel(at, base, info_ref, rate_ref, keep_ref, came_ref, out_ref):
    for h in range(out_ref.shape[0]):
        rate = rate_ref[base + h]
        mine = fade(rate, info_ref[at + 2], TILE)
        theirs = fade(rate, info_ref[at + 3], TILE)
        out_ref[h] = spread(mine, keep_ref[h]) + spread(theirs, came_ref[h])


def part_kernel(at, base, hops, first_side, info_ref, rate_ref, keep_ref, came_ref, *refs):
    moved, (own_ref, send_ref) = refs[:hops], refs[hops:]
    is_first = ((info_ref[INDEX] >> 1) & 1) == first_side
    for h in range(own_ref.shape[0]):
        rate = rate_ref[base + h]
        total = moved[0][h]
        for hop in range(1, hops):
            total += spread(fade(rate, info_ref[at + 5 + hop], TILE), moved[hop][h])
        earlier = jnp.where(is_first, keep_ref[h], came_ref[h])
        later = spread(fade(rate, info_ref[at + 4], TILE), total) + earlier
        own_ref[h] = jnp.where(is_first, total, later)
        send_ref[h] = jnp.where(is_first, later, total)


def half_kernel(at, base, first_core, info_ref, rate_ref, keep_ref, came_ref, own_ref, came_part_ref, mine_ref, send_ref):
    heads = own_ref.shape[0]
    index = info_ref[INDEX]
    is_first = (index & 1) == first_core
    low_side = ((index >> 1) & 1) == 0
    for h in range(heads):
        own, came = own_ref[h], came_part_ref[h]
        half = jnp.concatenate(
            [jnp.where(low_side, own, came), jnp.where(low_side, came, own)], axis=0
        )
        earlier = jnp.where(is_first, keep_ref[h], came_ref[h])
        later = spread(fade(rate_ref[base + h], info_ref[at + 5], TILE), half) + earlier
        mine_ref[h] = jnp.where(is_first, half, later).astype(BF16)
        send_ref[h] = jnp.where(is_first, later, half)


def state_kernel(docs_ref, rate_ref, k_ref, v_ref, kh_ref, vh_ref, send_ref, keep_ref):
    tokens, heads, dim = k_ref.shape
    first = pl.program_id(0) * heads
    index = lax.axis_index("ctx")
    end = (index + 1) * tokens

    def scan(j, carry):
        start, last = carry
        last = jnp.where(start <= end - 1, start, last)
        return (start + docs_ref[j], last)

    _, last = lax.fori_loop(0, docs_ref.shape[0], scan, (jnp.int32(0), jnp.int32(0)))
    row = column(tokens, dim)
    distance = jnp.where(
        row + index * tokens >= last, (tokens - 1 - row).astype(F32), F32(FAR)
    )
    turned_k = jnp.swapaxes(k_ref[...], 0, 1)
    turned_v = jnp.swapaxes(v_ref[...], 0, 1)
    kh_ref[pl.ds(first, heads)] = turned_k
    vh_ref[pl.ds(first, heads)] = turned_v
    core = index & 1
    for h in range(heads):
        tail = jnp.exp(-rate_ref[first + h] * distance)
        faded = (turned_k[h].astype(F32) * tail).astype(BF16)
        split_halves(core, dot(faded, turned_v[h], TN), send_ref, keep_ref, first + h)


def turn_kernel(q_ref, g_ref, qh_ref, gh_ref):
    heads = q_ref.shape[1]
    here = pl.ds(pl.program_id(0) * heads, heads)
    qh_ref[here] = jnp.swapaxes(q_ref[...], 0, 1)
    gh_ref[here] = jnp.swapaxes(g_ref[...], 0, 1)


def scores_kernel(first, rows, rate_ref, qh_ref, kh_ref, vh_ref, dist_ref, out_ref, probs_ref):
    heads, tokens, _ = out_ref.shape

    def head(h, carry):
        full = first + h
        rate = rate_ref[full]
        for low in range(0, tokens, rows):
            top = low + rows
            scores = dot(qh_ref[full, low:top, :], kh_ref[full, :top, :], NT)
            decay = jnp.exp(-rate * dist_ref[low:top, :top])
            probs = (scores * decay).astype(BF16)
            probs_ref[h, low:top, :top] = probs
            out_ref[h, low:top, :] = dot(probs, vh_ref[full, :top, :], NN).astype(BF16)
        return carry

    lax.fori_loop(0, heads, head, 0)


def attend_kernel(base, groups, begin, final, info_ref, rate_ref, qh_ref, gh_ref, gain_ref, mine_ref, other_ref, *refs):
    local_refs, refs = refs[:groups], refs[groups:]
    if not begin:
        sums_ref, refs = refs[0], refs[1:]
    attn_ref, state_ref, stats_ref = refs
    heads, tokens, dim = attn_ref.shape
    count = heads // groups
    core = info_ref[INDEX] & 1
    row = column(tokens, dim)
    distance = jnp.where(
        row + info_ref[BASE] < info_ref[NEXT_START], (row + 1).astype(F32), F32(FAR)
    )
    if begin:
        squares = jnp.zeros((tokens, dim), F32)
        cross = jnp.zeros((tokens, dim), F32)
    else:
        squares, cross = sums_ref[0], sums_ref[1]
    for h in range(heads):
        full = base + h
        put_halves(core, state_ref, h, mine_ref[h], other_ref[h])
        factor = jnp.exp(-rate_ref[full] * distance)
        near = local_refs[h // count][h % count].astype(F32)
        attn = near + factor * dot(qh_ref[full], state_ref[h], NN)
        attn_ref[h] = attn.astype(BF16)
        squares += attn * attn
        cross += gain_ref[full : full + 1, :] * gh_ref[full].astype(F32) * attn
    if final:
        stats_ref[0:1, :] = jnp.sum(jnp.swapaxes(squares, 0, 1), axis=0, keepdims=True)
        stats_ref[1:2, :] = jnp.sum(jnp.swapaxes(cross, 0, 1), axis=0, keepdims=True)
    else:
        stats_ref[0] = squares
        stats_ref[1] = cross


def norm_kernel(base, width, parts, info_ref, rate_ref, *refs):
    stats_refs, refs = refs[:parts], refs[parts:]
    attn_ref, gh_ref, qh_ref, gain_ref, grad_ref, send_ref, keep_ref = refs
    heads, tokens, dim = grad_ref.shape
    core = info_ref[INDEX] & 1
    stats = stats_refs[0][...]
    for ref in stats_refs[1:]:
        stats = stats + ref[...]
    squares, cross = stats[0:1, :], stats[1:2, :]
    inverse = 1.0 / jnp.sqrt(squares / width + EPSILON)
    scale = cross * inverse * inverse * inverse / width
    inverse = jnp.swapaxes(jnp.broadcast_to(inverse, (dim, tokens)), 0, 1)
    scale = jnp.swapaxes(jnp.broadcast_to(scale, (dim, tokens)), 0, 1)
    row = column(tokens, dim)
    distance = jnp.where(row + info_ref[BASE] < info_ref[LATER_START], row.astype(F32), F32(FAR))
    for h in range(heads):
        full = base + h
        gained = gain_ref[full : full + 1, :] * gh_ref[full].astype(F32)
        grad = (gained * inverse - attn_ref[h].astype(F32) * scale).astype(BF16)
        grad_ref[h] = grad
        lead = jnp.exp(-rate_ref[full] * distance)
        faded = (qh_ref[full].astype(F32) * lead).astype(BF16)
        split_halves(core, dot(faded, grad, TN), send_ref, keep_ref, h)


def grads_kernel(base, first, rows, info_ref, rate_ref, grad_ref, qh_ref, kh_ref, vh_ref, probs_ref, dist_ref, state_ref, dq_ref, dk_ref, dv_ref):
    heads, tokens, dim = dq_ref.shape
    row = column(tokens, dim)
    distance = jnp.where(
        row + info_ref[BASE] < info_ref[NEXT_START], (row + 1).astype(F32), F32(FAR)
    )

    def head(h, carry):
        near = first + h
        full = base + near
        rate = rate_ref[full]
        factor = jnp.exp(-rate * distance)
        dk = dv = None
        for low in range(tokens - rows, -1, -rows):
            top = low + rows
            grad = grad_ref[near, low:top, :]
            raw = dot(grad, vh_ref[full, :top, :], NT)
            weights = (raw * jnp.exp(-rate * dist_ref[low:top, :top])).astype(BF16)
            dq = dot(weights, kh_ref[full, :top, :], NN)
            dq += factor[low:top] * dot(grad, state_ref[near], NT)
            dq_ref[h, low:top, :] = dq.astype(BF16)
            dk_new = dot(weights, qh_ref[full, low:top, :], TN)
            dv_new = dot(probs_ref[h, low:top, :top], grad, TN)
            if dk is not None:
                dk_new += dk[:top]
                dv_new += dv[:top]
            dk, dv = dk_new, dv_new
            dk_ref[h, low:top, :] = dk[low:top].astype(BF16)
            dv_ref[h, low:top, :] = dv[low:top].astype(BF16)
        return carry

    lax.fori_loop(0, heads, head, 0)


def turn_back_kernel(steps, *refs):
    parts, out_ref = refs[:-1], refs[-1]
    each = len(parts) // steps
    for s in range(steps):

        @pl.when(pl.program_id(0) == s)
        def _():
            block = [ref[...] for ref in parts[s * each : (s + 1) * each]]
            out_ref[...] = jnp.swapaxes(jnp.concatenate(block, axis=0), 0, 1)


def finish_kernel(base, groups, steps, info_ref, rate_ref, kh_ref, vh_ref, mine_ref, other_ref, *refs):
    dk_parts, dv_parts = refs[: groups * steps], refs[groups * steps : 2 * groups * steps]
    dk_ref, dv_ref, state_ref = refs[-3:]
    heads = mine_ref.shape[0]
    count, tokens, dim = dk_parts[0].shape
    core = info_ref[INDEX] & 1
    row = column(tokens, dim)
    distance = jnp.where(
        row + info_ref[BASE] >= info_ref[NEXT_BEGIN], (tokens - row).astype(F32), F32(FAR)
    )

    def block(first, dk_parts, dv_parts):
        dks, dvs = [], []
        for h in range(heads):
            full = first + h
            put_halves(core, state_ref, h, mine_ref[h], other_ref[h])
            factor = jnp.exp(-rate_ref[full] * distance)
            dk = dk_parts[h // count][h % count].astype(F32)
            dv = dv_parts[h // count][h % count].astype(F32)
            dk += factor * dot(vh_ref[full], state_ref[h], NT)
            dv += factor * dot(kh_ref[full], state_ref[h], NN)
            dks.append(dk.astype(BF16))
            dvs.append(dv.astype(BF16))
        dk_ref[...] = jnp.swapaxes(jnp.stack(dks), 0, 1)
        dv_ref[...] = jnp.swapaxes(jnp.stack(dvs), 0, 1)

    if base is not None:
        return block(base, dk_parts, dv_parts)
    for s in range(steps):
        here = slice(s * groups, (s + 1) * groups)
        pl.when(pl.program_id(0) == s)(partial(block, s * heads, dk_parts[here], dv_parts[here]))


def send(block, axis, target):
    count = lax.axis_size(axis)
    route = [(i, target(i)) for i in range(count) if 0 <= target(i) < count]
    return lax.ppermute(block, axis, route)


def hop_count(tokens):
    return -(-LONGEST // (4 * tokens))


def entering_state(leave, keep, info, rates, base, forward, hops):
    heads, rows, dim = keep.shape
    at = FADES + (0 if forward else len(fade_rows(hops)[0]))
    first = 0 if forward else 1
    step = 4 if forward else -4
    part = jax.ShapeDtypeStruct((heads, rows // 2, dim), F32)
    half = jax.ShapeDtypeStruct(keep.shape, F32)

    def combine(kernel, arrays, outs):
        return run(
            kernel,
            [info, rates, *arrays],
            [SMEM, SMEM] + [VMEM] * len(arrays),
            outs,
            [VMEM] * len(outs),
            cost=(0, 4 * heads * rows * dim),
        )

    came_half = send(leave, "ctx", lambda i: i ^ 1)
    keep_part, send_part = combine(partial(chip_kernel, at, base), [keep, came_half], [part] * 2)
    came_part = send(send_part, "ctx", lambda i: i ^ 2)
    (moving,) = combine(partial(plane_kernel, at, base), [keep_part, came_part], [part])
    moved = []
    for _ in range(hops):
        moving = send(moving, "ctx", lambda i: i + step)
        moved.append(moving)
    own, send_part = combine(
        partial(part_kernel, at, base, hops, first), [keep_part, came_part, *moved], [part] * 2
    )
    came = send(send_part, "ctx", lambda i: i ^ 2)
    mine, send_half = combine(
        partial(half_kernel, at, base, first),
        [keep, came_half, own, came],
        [jax.ShapeDtypeStruct(keep.shape, BF16), half],
    )
    return mine, send(send_half, "ctx", lambda i: i ^ 1)


def head_sum_parts(stats):
    count = lax.axis_size("head")
    if count & (count - 1):
        return [stats] + [
            lax.ppermute(stats, "head", [(i, (i + d) % count) for i in range(count)])
            for d in range(1, count)
        ]
    parts, bit = [stats], 1
    while bit < count:
        stats = parts[0] if len(parts) == 1 else parts[0] + parts[1]
        parts = [stats, send(stats, "head", lambda i: i ^ bit)]
        bit *= 2
    return parts


SMEM = pl.BlockSpec(memory_space=pltpu.SMEM)
VMEM = pl.BlockSpec(memory_space=pltpu.VMEM)


def kept(*arrays):
    return [pltpu.with_memory_space_constraint(a, pltpu.VMEM) for a in arrays]


def at_hand(*arrays):
    return [pltpu.with_memory_space_constraint(a, pltpu.SMEM) for a in arrays]


def streamed(*arrays):
    return [pltpu.with_memory_space_constraint(a, pltpu.HBM) for a in arrays]


def run(kernel, args, specs, outs, out_specs, steps=None, scratch=(), alias=None, cost=(0, 0)):
    return pl.pallas_call(
        kernel,
        out_shape=outs,
        grid=() if steps is None else (steps,),
        in_specs=specs,
        out_specs=out_specs,
        scratch_shapes=scratch,
        input_output_aliases=alias or {},
        cost_estimate=pl.CostEstimate(flops=cost[0], bytes_accessed=cost[1], transcendentals=0),
        compiler_params=pltpu.CompilerParams(vmem_limit_bytes=16 << 20),
    )(*args)


def body(queries, keys, values, out_grad, gain, rates, docs):
    tokens, heads, dim = queries.shape
    wide = 8 if heads % 8 == 0 else heads
    count = 4 if wide % 4 == 0 else wide
    span = heads // (CHUNKS if heads % (CHUNKS * count) == 0 else 1)
    steps, groups = heads // wide, span // count
    total_groups = heads // count
    rows = tokens // 2
    hops = hop_count(tokens)
    width = heads * dim * lax.axis_size("head")
    chunks = range(heads // span)
    last = heads // span - 1
    shape = lambda *s: jax.ShapeDtypeStruct(s, F32)
    major = pltpu.VMEM((heads, tokens, dim), BF16)
    chunk = pltpu.VMEM((span, tokens, dim), BF16)
    some = pltpu.VMEM((count, tokens, dim), BF16)
    half = shape(span, dim // 2, dim)
    token_block = pl.BlockSpec((tokens, wide, dim), lambda i: (0, i, 0))
    unit = heads * tokens * dim
    rates, docs, gain = streamed(rates, docs, gain)

    kh, vh, leave, keep = run(
        state_kernel,
        [docs, rates, *streamed(keys, values)],
        [SMEM, SMEM, token_block, token_block],
        [major, major] + [shape(heads, dim // 2, dim)] * 2,
        [VMEM] * 4,
        steps=steps,
        cost=(2 * unit * dim, 8 * unit),
    )

    halves = [x[c * span : (c + 1) * span] for c in chunks for x in (leave, keep)]

    spans = sum(len(rows) for rows in fade_rows(hops))
    info, rates = run(
        partial(setup_kernel, hops, tokens),
        [docs, rates],
        [SMEM] * 2,
        [pltpu.SMEM((FADES + spans,), jnp.int32), pltpu.SMEM((heads,), F32)],
        [SMEM] * 2,
    )
    info, rates = at_hand(info, rates)
    distance = run(
        mask_kernel,
        [docs],
        [SMEM],
        pltpu.VMEM((tokens, tokens), F32),
        VMEM,
        scratch=[pltpu.VMEM((tokens, dim), jnp.int32)],
        cost=(0, 2 * tokens * tokens),
    )

    qh, gh = run(
        turn_kernel,
        streamed(queries, out_grad),
        [token_block, token_block],
        [major, major],
        [VMEM, VMEM],
        steps=steps,
        cost=(0, 8 * unit),
    )
    near, probs = [], []
    for g in range(total_groups):
        n, p = run(
            partial(scores_kernel, g * count, rows),
            [rates, *kept(qh, kh, vh, distance)],
            [SMEM] + [VMEM] * 4,
            [some, pltpu.VMEM((count, tokens, tokens), BF16)],
            [VMEM] * 2,
            cost=(4 * unit * tokens // total_groups, 0),
        )
        near.append(n), probs.append(p)

    attn, states, stats = [], [], None
    for c in chunks:
        mine, other = entering_state(*halves[2 * c : 2 * c + 2], info, rates, c * span, True, hops)
        begin, final = c == 0, c == last
        args = [info, rates, *kept(qh, gh), gain, mine, other, *kept(*near[c * groups : (c + 1) * groups])]
        if not begin:
            args += kept(stats)
        a, s, stats = run(
            partial(attend_kernel, c * span, groups, begin, final),
            args,
            [SMEM, SMEM] + [VMEM] * (len(args) - 2),
            [
                chunk,
                pltpu.VMEM((span, dim, dim), BF16),
                shape(2, tokens) if final else pltpu.VMEM((2, tokens, dim), F32),
            ],
            [VMEM] * 3,
            cost=(2 * unit * dim // len(chunks), 0),
        )
        attn.append(a), states.append(s)
    parts = head_sum_parts(stats)

    grads, halves = [], []
    for c in chunks:
        g, *pair = run(
            partial(norm_kernel, c * span, width, len(parts)),
            [info, rates, *parts, *kept(attn[c], gh, qh), gain],
            [SMEM, SMEM] + [VMEM] * (len(parts) + 4),
            [chunk, half, half],
            [VMEM] * 3,
            cost=(2 * unit * dim // len(chunks), 0),
        )
        grads.append(g), halves.extend(pair)

    dqh, dk_part, dv_part = [], [], []
    for g in range(total_groups):
        c, at = divmod(g, groups)
        parts = run(
            partial(grads_kernel, c * span, at * count, rows),
            [info, rates, *kept(grads[c], qh, kh, vh, probs[g], distance, states[c])],
            [SMEM, SMEM] + [VMEM] * 7,
            [some] * 3,
            [VMEM] * 3,
            cost=(8 * unit * tokens // total_groups, 0),
        )
        for kind, part in zip((dqh, dk_part, dv_part), parts):
            kind.append(part)
    full = jax.ShapeDtypeStruct((tokens, heads, dim), BF16)
    dq = run(
        partial(turn_back_kernel, steps),
        kept(*dqh),
        [VMEM] * total_groups,
        full,
        token_block,
        steps=steps,
        cost=(0, 2 * unit),
    )

    entered = [
        entering_state(*halves[2 * c : 2 * c + 2], info, rates, c * span, False, hops)
        for c in chunks
    ]
    made = []
    if len(chunks) == 1:
        ((mine, other),) = entered
        half_block = pl.BlockSpec((wide, dim // 2, dim), lambda i: (i, 0, 0))
        made = run(
            partial(finish_kernel, None, total_groups // steps, steps),
            [info, rates, *kept(kh, vh), mine, other, *kept(*dk_part, *dv_part)],
            [SMEM, SMEM, VMEM, VMEM, half_block, half_block] + [VMEM] * (2 * total_groups),
            [full, full],
            [token_block, token_block],
            steps=steps,
            scratch=[pltpu.VMEM((wide, dim, dim), BF16)],
            cost=(4 * unit * dim, 4 * unit),
        )
        return dq, *made
    for c in chunks:
        mine, other = entered[c]
        here = slice(c * groups, (c + 1) * groups)
        args = [info, rates, *kept(kh, vh), mine, other, *kept(*dk_part[here], *dv_part[here])]
        specs = [SMEM, SMEM] + [VMEM] * (4 + 2 * groups)
        alias = {len(args) + j: j for j in range(len(made))}
        block = pl.BlockSpec((tokens, wide, dim), lambda i, c=c: (0, c, 0))
        made = run(
            partial(finish_kernel, c * span, groups, 1),
            args + list(made),
            specs + [pl.BlockSpec(memory_space=pl.ANY)] * len(made),
            [full, full],
            [block, block],
            steps=1,
            scratch=[pltpu.VMEM((wide, dim, dim), BF16)],
            alias=alias,
            cost=(4 * unit * dim // len(chunks), 4 * unit // len(chunks)),
        )
    return dq, *made


def solution(mesh):
    token, head = P("ctx", "head", None), P("head")
    return jax.shard_map(
        body,
        mesh=mesh,
        in_specs=(token, token, token, token, P("head", None), head, P()),
        out_specs=(token, token, token),
        check_vma=False,
    )
```

```python
from functools import partial

import jax
import jax.numpy as jnp
from jax import lax
from jax.experimental import pallas as pl
from jax.experimental.pallas import tpu as pltpu
from jax.sharding import PartitionSpec as P


EPSILON = 1e-06
LONGEST = 4096
FAR = 1e30
APART = 1 << 30
CHUNKS = 2
F32 = jnp.float32
BF16 = jnp.bfloat16


def dot(left, right, dims):
    return lax.dot_general(left, right, (dims, ((), ())), preferred_element_type=F32)


NN = ((1,), (0,))
NT = ((1,), (1,))
TN = ((0,), (0,))


def column(tokens, width):
    return lax.broadcasted_iota(jnp.int32, (tokens, width), 0)


def put_halves(core, ref, h, mine, other):
    half = mine.shape[0]
    ref[h, pl.ds(pl.multiple_of(core * half, half), half), :] = mine.astype(ref.dtype)
    ref[h, pl.ds(pl.multiple_of((1 - core) * half, half), half), :] = other.astype(ref.dtype)


def split_halves(core, state, send_ref, keep_ref, h):
    half = state.shape[0] // 2
    low, high = state[:half], state[half:]
    keep_ref[h] = jnp.where(core == 0, low, high)
    send_ref[h] = jnp.where(core == 0, high, low)


INDEX, BASE, NEXT_START, LATER_START, NEXT_BEGIN = range(5)
MID_NEXT, MID_LATER, MID_BEGIN, MID_AHEAD, MID_OWN, MID_BACK, FADES = range(5, 12)


def fade_rows(hops):
    c, p = ~1, ~3
    ahead = [
        (0, -1, 1, 0, c, 2),
        (1, -1, 1, 0, c, 2),
        (0, c, 2, 0, p, 4),
        (2, c, 2, 0, p, 4),
        (0, p, 0, 0, p, 2),
        (0, c, 0, 0, c, 1),
    ]
    back = [
        (0, -1, 0, 0, c, 0),
        (1, -1, 0, 0, c, 0),
        (0, c, 0, 0, p, 0),
        (2, c, 0, 0, p, 0),
        (0, p, 4, 0, p, 2),
        (0, c, 2, 0, c, 1),
    ]
    ahead += [(0, p, -4 * hop, 0, p, 0) for hop in range(1, hops)]
    back += [(0, p, 4 + 4 * hop, 0, p, 4) for hop in range(1, hops)]
    return ahead, back


def setup_kernel(hops, tokens, docs_ref, rate_in_ref, info_ref, rate_ref):
    for h in range(rate_ref.shape[0]):
        rate_ref[h] = rate_in_ref[h]
    index = lax.axis_index("ctx").astype(jnp.int32)
    base = index * tokens
    ahead, back = fade_rows(hops)
    spot = lambda x, a, d: (((index ^ x) & a) + d) * tokens
    spans = [(spot(*row[:3]), spot(*row[3:])) for row in ahead + back]
    tops = [end - 1 for _, end in spans[: len(ahead)]] + [begin for begin, _ in spans[len(ahead) :]]
    mid, top = base + tokens // 2, base + tokens
    tops += [mid, top]

    def doc(j, carry):
        start, upper, later, mid_next, mid_later, seen = carry
        upper = jnp.where((start >= base) & (start < upper), start, upper)
        later = jnp.where((start > base) & (start < later), start, later)
        mid_next = jnp.where((start >= mid) & (start < mid_next), start, mid_next)
        mid_later = jnp.where((start > mid) & (start < mid_later), start, mid_later)
        seen = tuple(jnp.where(start <= top, start, old) for top, old in zip(tops, seen))
        return start + docs_ref[j], upper, later, mid_next, mid_later, seen

    zero = jnp.int32(0)
    far = jnp.int32(APART)
    _, upper, later, mid_next, mid_later, seen = lax.fori_loop(
        0, docs_ref.shape[0], doc, (zero, far, far, far, far, (zero,) * len(tops))
    )
    info_ref[INDEX] = index
    info_ref[BASE] = base
    info_ref[NEXT_START] = upper
    info_ref[LATER_START] = later
    info_ref[NEXT_BEGIN] = seen[-1]
    info_ref[MID_NEXT] = mid_next
    info_ref[MID_LATER] = mid_later
    info_ref[MID_BEGIN] = seen[-2]
    across = jnp.int32(tokens // 2)
    info_ref[MID_AHEAD] = jnp.where(upper >= mid, across, far)
    info_ref[MID_OWN] = jnp.where(later > mid, across, far)
    info_ref[MID_BACK] = jnp.where(mid_later > top, across, far)
    for j, ((begin, end), last) in enumerate(zip(spans, seen)):
        forward = j < len(ahead)
        joined = last < begin if forward else last <= end
        info_ref[FADES + j] = jnp.where(joined, end - begin if forward else begin - end, far)


def mask_kernel(docs_ref, dist_ref, begin_ref):
    tokens, lanes = begin_ref.shape
    base = lax.axis_index("ctx").astype(jnp.int32) * tokens
    row = column(tokens, lanes)
    begin_ref[...] = jnp.zeros_like(begin_ref)

    def doc(j, start):
        @pl.when((start > base) & (start < base + tokens))
        def _():
            begin_ref[...] = jnp.where(row >= start - base, start - base, begin_ref[...])

        return start + docs_ref[j]

    lax.fori_loop(0, docs_ref.shape[0], doc, jnp.int32(0))
    side = tokens // 2
    across = jnp.where(row >= side, side, 0)
    for low in range(0, side, lanes):
        spots = across + low + lax.broadcasted_iota(jnp.int32, (tokens, lanes), 1)
        allowed = (spots <= row) & (spots >= begin_ref[...])
        dist_ref[:, low : low + lanes] = jnp.where(allowed, (row - spots).astype(F32), F32(FAR))


def fade(rate, distance, shape):
    return jnp.exp(jnp.full(shape, -rate * distance.astype(F32), F32))


def spread(factor, block):
    return (block.reshape(-1, *factor.shape) * factor[None]).reshape(block.shape)


TILE = (8, 128)


def chip_kernel(at, base, info_ref, rate_ref, keep_ref, came_ref, keep_part_ref, send_part_ref):
    heads, quarter, _ = keep_part_ref.shape
    side = (info_ref[INDEX] >> 1) & 1
    for h in range(heads):
        rate = rate_ref[base + h]
        mine = fade(rate, info_ref[at], TILE)
        theirs = fade(rate, info_ref[at + 1], TILE)
        chip = spread(mine, keep_ref[h]) + spread(theirs, came_ref[h])
        low, high = chip[:quarter], chip[quarter:]
        keep_part_ref[h] = jnp.where(side == 0, low, high)
        send_part_ref[h] = jnp.where(side == 0, high, low)


def plane_kernel(at, base, info_ref, rate_ref, keep_ref, came_ref, out_ref):
    for h in range(out_ref.shape[0]):
        rate = rate_ref[base + h]
        mine = fade(rate, info_ref[at + 2], TILE)
        theirs = fade(rate, info_ref[at + 3], TILE)
        out_ref[h] = spread(mine, keep_ref[h]) + spread(theirs, came_ref[h])


def part_kernel(at, base, hops, first_side, info_ref, rate_ref, keep_ref, came_ref, *refs):
    moved, (own_ref, send_ref) = refs[:hops], refs[hops:]
    is_first = ((info_ref[INDEX] >> 1) & 1) == first_side
    for h in range(own_ref.shape[0]):
        rate = rate_ref[base + h]
        total = moved[0][h]
        for hop in range(1, hops):
            total += spread(fade(rate, info_ref[at + 5 + hop], TILE), moved[hop][h])
        earlier = jnp.where(is_first, keep_ref[h], came_ref[h])
        later = spread(fade(rate, info_ref[at + 4], TILE), total) + earlier
        own_ref[h] = jnp.where(is_first, total, later)
        send_ref[h] = jnp.where(is_first, later, total)


def half_kernel(at, base, first_core, info_ref, rate_ref, keep_ref, came_ref, own_ref, came_part_ref, mine_ref, send_ref):
    heads = own_ref.shape[0]
    index = info_ref[INDEX]
    is_first = (index & 1) == first_core
    low_side = ((index >> 1) & 1) == 0
    for h in range(heads):
        own, came = own_ref[h], came_part_ref[h]
        half = jnp.concatenate(
            [jnp.where(low_side, own, came), jnp.where(low_side, came, own)], axis=0
        )
        earlier = jnp.where(is_first, keep_ref[h], came_ref[h])
        later = spread(fade(rate_ref[base + h], info_ref[at + 5], TILE), half) + earlier
        mine_ref[h] = jnp.where(is_first, half, later).astype(BF16)
        send_ref[h] = jnp.where(is_first, later, half)


def by_side(row, first, second):
    return jnp.where(row < row.shape[0] // 2, first, second)


def state_kernel(docs_ref, rate_ref, k_ref, v_ref, kh_ref, vh_ref, send_ref, keep_ref, half_ref):
    tokens, heads, dim = k_ref.shape
    side = tokens // 2
    first = pl.program_id(0) * heads
    index = lax.axis_index("ctx")
    base = index * tokens
    mid, end = base + side, base + tokens

    def scan(j, carry):
        start, mid_last, last = carry
        mid_last = jnp.where(start <= mid - 1, start, mid_last)
        last = jnp.where(start <= end - 1, start, last)
        return (start + docs_ref[j], mid_last, last)

    _, mid_last, last = lax.fori_loop(0, docs_ref.shape[0], scan, (jnp.int32(0),) * 3)
    across = jnp.where(last < mid, jnp.int32(side), jnp.int32(APART))
    row = column(tokens, dim)
    distance = jnp.where(
        row + base >= by_side(row, mid_last, last),
        (by_side(row, side, tokens) - 1 - row).astype(F32),
        F32(FAR),
    )
    turned_k = jnp.swapaxes(k_ref[...], 0, 1)
    turned_v = jnp.swapaxes(v_ref[...], 0, 1)
    kh_ref[pl.ds(first, heads)] = turned_k
    vh_ref[pl.ds(first, heads)] = turned_v
    core = index & 1
    for h in range(heads):
        rate = rate_ref[first + h]
        tail = jnp.exp(-rate * distance)
        faded = (turned_k[h].astype(F32) * tail).astype(BF16)
        near = dot(faded[:side], turned_v[h, :side], TN)
        half_ref[first + h] = near
        state = spread(fade(rate, across, TILE), near) + dot(faded[side:], turned_v[h, side:], TN)
        split_halves(core, state, send_ref, keep_ref, first + h)


def turn_kernel(q_ref, g_ref, qh_ref, gh_ref):
    heads = q_ref.shape[1]
    here = pl.ds(pl.program_id(0) * heads, heads)
    qh_ref[here] = jnp.swapaxes(q_ref[...], 0, 1)
    gh_ref[here] = jnp.swapaxes(g_ref[...], 0, 1)


def scores_kernel(first, rows, rate_ref, qh_ref, kh_ref, vh_ref, dist_ref, out_ref, probs_ref):
    heads, tokens, _ = out_ref.shape

    def head(h, carry):
        full = first + h
        rate = rate_ref[full]
        for low in range(0, tokens, rows):
            here = slice(low, low + rows)
            scores = dot(qh_ref[full, here, :], kh_ref[full, here, :], NT)
            probs = (scores * jnp.exp(-rate * dist_ref[here, :])).astype(BF16)
            probs_ref[h, here, :] = probs
            out_ref[h, here, :] = dot(probs, vh_ref[full, here, :], NN).astype(BF16)
        return carry

    lax.fori_loop(0, heads, head, 0, unroll=2 if heads % 2 == 0 else 1)


def entry_distance(info_ref, row):
    side = row.shape[0] // 2
    return jnp.where(
        row + info_ref[BASE] < by_side(row, info_ref[NEXT_START], info_ref[MID_NEXT]),
        (row + 1 - by_side(row, 0, side)).astype(F32),
        F32(FAR),
    )


def attend_kernel(groups, info_ref, rate_ref, qh_ref, gh_ref, gain_ref, mine_ref, other_ref, half_ref, *refs):
    local_refs, (attn_ref, state_ref, mid_ref, stats_ref) = refs[:groups], refs[groups:]
    heads, tokens, dim = attn_ref.shape
    side = tokens // 2
    count = heads // groups
    core = info_ref[INDEX] & 1
    distance = entry_distance(info_ref, column(tokens, dim))
    squares = jnp.zeros((tokens, dim), F32)
    cross = jnp.zeros((tokens, dim), F32)
    for h in range(heads):
        rate = rate_ref[h]
        put_halves(core, state_ref, h, mine_ref[h], other_ref[h])
        state = state_ref[h]
        mid = (spread(fade(rate, info_ref[MID_AHEAD], TILE), state.astype(F32)) + half_ref[h]).astype(BF16)
        mid_ref[h] = mid
        far = jnp.concatenate(
            [dot(qh_ref[h, :side, :], state, NN), dot(qh_ref[h, side:, :], mid, NN)], axis=0
        )
        near = local_refs[h // count][h % count].astype(F32)
        attn = near + jnp.exp(-rate * distance) * far
        attn_ref[h] = attn.astype(BF16)
        squares += attn * attn
        cross += gain_ref[h : h + 1, :] * gh_ref[h].astype(F32) * attn
    stats_ref[0:1, :] = jnp.sum(jnp.swapaxes(squares, 0, 1), axis=0, keepdims=True)
    stats_ref[1:2, :] = jnp.sum(jnp.swapaxes(cross, 0, 1), axis=0, keepdims=True)


def norm_kernel(base, width, parts, info_ref, rate_ref, *refs):
    stats_refs, refs = refs[:parts], refs[parts:]
    attn_ref, gh_ref, qh_ref, gain_ref, grad_ref, send_ref, keep_ref, half_ref = refs
    heads, tokens, dim = grad_ref.shape
    core = info_ref[INDEX] & 1
    stats = stats_refs[0][...]
    for ref in stats_refs[1:]:
        stats = stats + ref[...]
    squares, cross = stats[0:1, :], stats[1:2, :]
    inverse = 1.0 / jnp.sqrt(squares / width + EPSILON)
    scale = cross * inverse * inverse * inverse / width
    inverse = jnp.swapaxes(jnp.broadcast_to(inverse, (dim, tokens)), 0, 1)
    scale = jnp.swapaxes(jnp.broadcast_to(scale, (dim, tokens)), 0, 1)
    row = column(tokens, dim)
    side = tokens // 2
    distance = jnp.where(
        row + info_ref[BASE] < by_side(row, info_ref[LATER_START], info_ref[MID_LATER]),
        (row - by_side(row, 0, side)).astype(F32),
        F32(FAR),
    )
    for h in range(heads):
        full = base + h
        gained = gain_ref[full : full + 1, :] * gh_ref[full].astype(F32)
        grad = (gained * inverse - attn_ref[full].astype(F32) * scale).astype(BF16)
        grad_ref[h] = grad
        lead = jnp.exp(-rate_ref[full] * distance)
        faded = (qh_ref[full].astype(F32) * lead).astype(BF16)
        near = dot(faded[side:], grad[side:], TN)
        half_ref[h] = near
        state = dot(faded[:side], grad[:side], TN)
        state += spread(fade(rate_ref[full], info_ref[MID_OWN], TILE), near)
        split_halves(core, state, send_ref, keep_ref, h)


def grads_kernel(base, first, rows, info_ref, rate_ref, grad_ref, qh_ref, kh_ref, vh_ref, probs_ref, dist_ref, state_ref, mid_ref, dq_ref, dk_ref, dv_ref):
    heads, tokens, dim = dq_ref.shape
    distance = entry_distance(info_ref, column(tokens, dim))

    def head(h, carry):
        near = first + h
        full = base + near
        rate = rate_ref[full]
        factor = jnp.exp(-rate * distance)
        for low, entry_ref in ((0, state_ref), (rows, mid_ref)):
            here = slice(low, low + rows)
            grad = grad_ref[near, here, :]
            raw = dot(grad, vh_ref[full, here, :], NT)
            weights = (raw * jnp.exp(-rate * dist_ref[here, :])).astype(BF16)
            dq = dot(weights, kh_ref[full, here, :], NN)
            dq += factor[here] * dot(grad, entry_ref[full], NT)
            dq_ref[h, here, :] = dq.astype(BF16)
            dk_ref[h, here, :] = dot(weights, qh_ref[full, here, :], TN).astype(BF16)
            dv_ref[h, here, :] = dot(probs_ref[h, here, :], grad, TN).astype(BF16)
        return carry

    lax.fori_loop(0, heads, head, 0, unroll=2 if heads % 2 == 0 else 1)


def turn_back_kernel(steps, *refs):
    parts, out_ref = refs[:-1], refs[-1]
    each = len(parts) // steps
    for s in range(steps):

        @pl.when(pl.program_id(0) == s)
        def _():
            block = [ref[...] for ref in parts[s * each : (s + 1) * each]]
            out_ref[...] = jnp.swapaxes(jnp.concatenate(block, axis=0), 0, 1)


def finish_kernel(base, groups, steps, info_ref, rate_ref, kh_ref, vh_ref, mine_ref, other_ref, half_ref, *refs):
    dk_parts, dv_parts = refs[: groups * steps], refs[groups * steps : 2 * groups * steps]
    dk_ref, dv_ref, state_ref = refs[-3:]
    heads = mine_ref.shape[0]
    count, tokens, dim = dk_parts[0].shape
    core = info_ref[INDEX] & 1
    row = column(tokens, dim)
    side = tokens // 2
    distance = jnp.where(
        row + info_ref[BASE] >= by_side(row, info_ref[MID_BEGIN], info_ref[NEXT_BEGIN]),
        (by_side(row, side, tokens) - row).astype(F32),
        F32(FAR),
    )

    def block(first, dk_parts, dv_parts):
        dks, dvs = [], []
        for h in range(heads):
            full = first + h
            put_halves(core, state_ref, h, mine_ref[h], other_ref[h])
            factor = jnp.exp(-rate_ref[full] * distance)
            dk = dk_parts[h // count][h % count].astype(F32)
            dv = dv_parts[h // count][h % count].astype(F32)
            state = state_ref[h]
            faded = spread(fade(rate_ref[full], info_ref[MID_BACK], TILE), state.astype(F32))
            mid = (faded + half_ref[h]).astype(BF16)
            v, k = vh_ref[full], kh_ref[full]
            dk += factor * jnp.concatenate([dot(v[:side], mid, NT), dot(v[side:], state, NT)], axis=0)
            dv += factor * jnp.concatenate([dot(k[:side], mid, NN), dot(k[side:], state, NN)], axis=0)
            dks.append(dk.astype(BF16))
            dvs.append(dv.astype(BF16))
        dk_ref[...] = jnp.swapaxes(jnp.stack(dks), 0, 1)
        dv_ref[...] = jnp.swapaxes(jnp.stack(dvs), 0, 1)

    if base is not None:
        return block(base, dk_parts, dv_parts)
    for s in range(steps):
        here = slice(s * groups, (s + 1) * groups)
        pl.when(pl.program_id(0) == s)(partial(block, s * heads, dk_parts[here], dv_parts[here]))


def send(block, axis, target):
    count = lax.axis_size(axis)
    route = [(i, target(i)) for i in range(count) if 0 <= target(i) < count]
    return lax.ppermute(block, axis, route)


def hop_count(tokens):
    return -(-LONGEST // (4 * tokens))


def entering_state(leave, keep, info, rates, base, forward, hops):
    heads, rows, dim = keep.shape
    at = FADES + (0 if forward else len(fade_rows(hops)[0]))
    first = 0 if forward else 1
    step = 4 if forward else -4
    part = jax.ShapeDtypeStruct((heads, rows // 2, dim), F32)
    half = jax.ShapeDtypeStruct(keep.shape, F32)

    def combine(kernel, arrays, outs):
        return run(
            kernel,
            [info, rates, *arrays],
            [SMEM, SMEM] + [VMEM] * len(arrays),
            outs,
            [VMEM] * len(outs),
            cost=(0, 4 * heads * rows * dim),
        )

    came_half = send(leave, "ctx", lambda i: i ^ 1)
    keep_part, send_part = combine(partial(chip_kernel, at, base), [keep, came_half], [part] * 2)
    came_part = send(send_part, "ctx", lambda i: i ^ 2)
    (moving,) = combine(partial(plane_kernel, at, base), [keep_part, came_part], [part])
    moved = []
    for _ in range(hops):
        moving = send(moving, "ctx", lambda i: i + step)
        moved.append(moving)
    own, send_part = combine(partial(part_kernel, at, base, hops, first), [keep_part, came_part, *moved], [part] * 2)
    came = send(send_part, "ctx", lambda i: i ^ 2)
    mine, send_half = combine(
        partial(half_kernel, at, base, first),
        [keep, came_half, own, came],
        [jax.ShapeDtypeStruct(keep.shape, BF16), half],
    )
    return mine, send(send_half, "ctx", lambda i: i ^ 1)


def head_sum_parts(stats):
    count = lax.axis_size("head")
    if count & (count - 1):
        return [stats] + [
            lax.ppermute(stats, "head", [(i, (i + d) % count) for i in range(count)])
            for d in range(1, count)
        ]
    parts, bit = [stats], 1
    while bit < count:
        stats = parts[0] if len(parts) == 1 else parts[0] + parts[1]
        parts = [stats, send(stats, "head", lambda i: i ^ bit)]
        bit *= 2
    return parts


SMEM = pl.BlockSpec(memory_space=pltpu.SMEM)
VMEM = pl.BlockSpec(memory_space=pltpu.VMEM)


def kept(*arrays):
    return [pltpu.with_memory_space_constraint(a, pltpu.VMEM) for a in arrays]


def at_hand(*arrays):
    return [pltpu.with_memory_space_constraint(a, pltpu.SMEM) for a in arrays]


def streamed(*arrays):
    return [pltpu.with_memory_space_constraint(a, pltpu.HBM) for a in arrays]


def run(kernel, args, specs, outs, out_specs, steps=None, scratch=(), alias=None, cost=(0, 0)):
    return pl.pallas_call(
        kernel,
        out_shape=outs,
        grid=() if steps is None else (steps,),
        in_specs=specs,
        out_specs=out_specs,
        scratch_shapes=scratch,
        input_output_aliases=alias or {},
        cost_estimate=pl.CostEstimate(flops=cost[0], bytes_accessed=cost[1], transcendentals=0),
        compiler_params=pltpu.CompilerParams(vmem_limit_bytes=16 << 20),
    )(*args)


def body(queries, keys, values, out_grad, gain, rates, docs):
    tokens, heads, dim = queries.shape
    wide = 8 if heads % 8 == 0 else heads
    count = 4 if wide % 4 == 0 else wide
    span = heads // (CHUNKS if heads % (CHUNKS * count) == 0 else 1)
    steps, groups = heads // wide, span // count
    total_groups = heads // count
    rows = tokens // 2
    hops = hop_count(tokens)
    width = heads * dim * lax.axis_size("head")
    chunks = range(heads // span)
    shape = lambda *s: jax.ShapeDtypeStruct(s, F32)
    major = pltpu.VMEM((heads, tokens, dim), BF16)
    chunk = pltpu.VMEM((span, tokens, dim), BF16)
    some = pltpu.VMEM((count, tokens, dim), BF16)
    half = shape(span, dim // 2, dim)
    token_block = pl.BlockSpec((tokens, wide, dim), lambda i: (0, i, 0))
    unit = heads * tokens * dim
    rates, docs, gain = streamed(rates, docs, gain)

    kh, vh, leave, keep, early = run(
        state_kernel,
        [docs, rates, *streamed(keys, values)],
        [SMEM, SMEM, token_block, token_block],
        [major, major] + [shape(heads, dim // 2, dim)] * 2 + [pltpu.VMEM((heads, dim, dim), F32)],
        [VMEM] * 5,
        steps=steps,
        cost=(2 * unit * dim, 8 * unit),
    )

    spans = sum(len(rows) for rows in fade_rows(hops))
    info, rates = run(
        partial(setup_kernel, hops, tokens),
        [docs, rates],
        [SMEM] * 2,
        [pltpu.SMEM((FADES + spans,), jnp.int32), pltpu.SMEM((heads,), F32)],
        [SMEM] * 2,
    )
    info, rates = at_hand(info, rates)
    distance = run(
        mask_kernel,
        [docs],
        [SMEM],
        pltpu.VMEM((tokens, rows), F32),
        VMEM,
        scratch=[pltpu.VMEM((tokens, dim), jnp.int32)],
        cost=(0, 2 * tokens * tokens),
    )

    qh, gh = run(
        turn_kernel,
        streamed(queries, out_grad),
        [token_block, token_block],
        [major, major],
        [VMEM, VMEM],
        steps=steps,
        cost=(0, 8 * unit),
    )
    near, probs = [], []
    for g in range(total_groups):
        n, p = run(
            partial(scores_kernel, g * count, rows),
            [rates, *kept(qh, kh, vh, distance)],
            [SMEM] + [VMEM] * 4,
            [some, pltpu.VMEM((count, tokens, rows), BF16)],
            [VMEM] * 2,
            cost=(4 * unit * tokens // total_groups, 0),
        )
        near.append(n), probs.append(p)

    mine, other = entering_state(leave, keep, info, rates, 0, True, hops)
    states = pltpu.VMEM((heads, dim, dim), BF16)
    attn, states, mids, stats = run(
        partial(attend_kernel, total_groups),
        [info, rates, *kept(qh, gh), gain, mine, other, *kept(early, *near)],
        [SMEM, SMEM] + [VMEM] * (6 + total_groups),
        [major, states, states, shape(2, tokens)],
        [VMEM] * 4,
        cost=(2 * unit * dim, 0),
    )
    parts = head_sum_parts(stats)

    grads, halves, late = [], [], []
    for c in chunks:
        g, *pair, n = run(
            partial(norm_kernel, c * span, width, len(parts)),
            [info, rates, *parts, *kept(attn, gh, qh), gain],
            [SMEM, SMEM] + [VMEM] * (len(parts) + 4),
            [chunk, half, half, pltpu.VMEM((span, dim, dim), F32)],
            [VMEM] * 4,
            cost=(2 * unit * dim // len(chunks), 0),
        )
        grads.append(g), halves.extend(pair), late.append(n)

    dqh, dk_part, dv_part = [], [], []
    for g in range(total_groups):
        c, at = divmod(g, groups)
        parts = run(
            partial(grads_kernel, c * span, at * count, rows),
            [info, rates, *kept(grads[c], qh, kh, vh, probs[g], distance, states, mids)],
            [SMEM, SMEM] + [VMEM] * 8,
            [some] * 3,
            [VMEM] * 3,
            cost=(8 * unit * tokens // total_groups, 0),
        )
        for kind, part in zip((dqh, dk_part, dv_part), parts):
            kind.append(part)
    full = jax.ShapeDtypeStruct((tokens, heads, dim), BF16)
    dq = run(
        partial(turn_back_kernel, steps),
        kept(*dqh),
        [VMEM] * total_groups,
        full,
        token_block,
        steps=steps,
        cost=(0, 2 * unit),
    )

    entered = [entering_state(*halves[2 * c : 2 * c + 2], info, rates, c * span, False, hops) for c in chunks]
    made = []
    if len(chunks) == 1:
        ((mine, other),) = entered
        half_block = pl.BlockSpec((wide, dim // 2, dim), lambda i: (i, 0, 0))
        full_block = pl.BlockSpec((wide, dim, dim), lambda i: (i, 0, 0))
        made = run(
            partial(finish_kernel, None, total_groups // steps, steps),
            [info, rates, *kept(kh, vh), mine, other, late[0], *kept(*dk_part, *dv_part)],
            [SMEM, SMEM, VMEM, VMEM, half_block, half_block, full_block] + [VMEM] * (2 * total_groups),
            [full, full],
            [token_block, token_block],
            steps=steps,
            scratch=[pltpu.VMEM((wide, dim, dim), BF16)],
            cost=(4 * unit * dim, 4 * unit),
        )
        return dq, *made
    for c in chunks:
        mine, other = entered[c]
        here = slice(c * groups, (c + 1) * groups)
        args = [info, rates, *kept(kh, vh), mine, other, *kept(late[c], *dk_part[here], *dv_part[here])]
        specs = [SMEM, SMEM] + [VMEM] * (5 + 2 * groups)
        alias = {len(args) + j: j for j in range(len(made))}
        block = pl.BlockSpec((tokens, wide, dim), lambda i, c=c: (0, c, 0))
        made = run(
            partial(finish_kernel, c * span, groups, 1),
            args + list(made),
            specs + [pl.BlockSpec(memory_space=pl.ANY)] * len(made),
            [full, full],
            [block, block],
            steps=1,
            scratch=[pltpu.VMEM((wide, dim, dim), BF16)],
            alias=alias,
            cost=(4 * unit * dim // len(chunks), 4 * unit // len(chunks)),
        )
    return dq, *made


def solution(mesh):
    token, head = P("ctx", "head", None), P("head")
    return jax.shard_map(
        body,
        mesh=mesh,
        in_specs=(token, token, token, token, P("head", None), head, P()),
        out_specs=(token, token, token),
        check_vma=False,
    )
```

```python
from functools import partial

import jax
import jax.numpy as jnp
from jax import lax
from jax.experimental import pallas as pl
from jax.experimental.pallas import tpu as pltpu
from jax.sharding import PartitionSpec as P


EPSILON = 1e-06
LONGEST = 4096
FAR = 1e30
APART = 1 << 30
F32 = jnp.float32
BF16 = jnp.bfloat16


def dot(left, right, dims):
    return lax.dot_general(left, right, (dims, ((), ())), preferred_element_type=F32)


NN = ((1,), (0,))
NT = ((1,), (1,))
TN = ((0,), (0,))


def column(tokens, width):
    return lax.broadcasted_iota(jnp.int32, (tokens, width), 0)


def put_halves(core, ref, h, mine, other):
    half = mine.shape[0]
    ref[h, pl.ds(pl.multiple_of(core * half, half), half), :] = mine.astype(ref.dtype)
    ref[h, pl.ds(pl.multiple_of((1 - core) * half, half), half), :] = other.astype(ref.dtype)


def split_halves(core, state, send_ref, keep_ref, h):
    half = state.shape[0] // 2
    low, high = state[:half], state[half:]
    keep_ref[h] = jnp.where(core == 0, low, high)
    send_ref[h] = jnp.where(core == 0, high, low)


INDEX, BASE, NEXT_START, LATER_START, NEXT_BEGIN = range(5)
MID_NEXT, MID_LATER, MID_BEGIN, MID_AHEAD, MID_OWN, MID_BACK, FADES = range(5, 12)


def fade_rows(hops):
    c, p = ~1, ~3
    ahead = [
        (0, -1, 1, 0, c, 2),
        (1, -1, 1, 0, c, 2),
        (0, c, 2, 0, p, 4),
        (2, c, 2, 0, p, 4),
        (0, p, 0, 0, p, 2),
        (0, c, 0, 0, c, 1),
    ]
    back = [
        (0, -1, 0, 0, c, 0),
        (1, -1, 0, 0, c, 0),
        (0, c, 0, 0, p, 0),
        (2, c, 0, 0, p, 0),
        (0, p, 4, 0, p, 2),
        (0, c, 2, 0, c, 1),
    ]
    ahead += [(0, p, -4 * hop, 0, p, 0) for hop in range(1, hops)]
    back += [(0, p, 4 + 4 * hop, 0, p, 4) for hop in range(1, hops)]
    return ahead, back


def setup_kernel(hops, tokens, docs_ref, rate_in_ref, info_ref, rate_ref):
    for h in range(rate_ref.shape[0]):
        rate_ref[h] = rate_in_ref[h]
    index = lax.axis_index("ctx").astype(jnp.int32)
    base = index * tokens
    ahead, back = fade_rows(hops)
    spot = lambda x, a, d: (((index ^ x) & a) + d) * tokens
    spans = [(spot(*row[:3]), spot(*row[3:])) for row in ahead + back]
    tops = [end - 1 for _, end in spans[: len(ahead)]] + [begin for begin, _ in spans[len(ahead) :]]
    mid, top = base + tokens // 2, base + tokens
    tops += [mid, top]

    def doc(j, carry):
        start, upper, later, mid_next, mid_later, seen = carry
        upper = jnp.where((start >= base) & (start < upper), start, upper)
        later = jnp.where((start > base) & (start < later), start, later)
        mid_next = jnp.where((start >= mid) & (start < mid_next), start, mid_next)
        mid_later = jnp.where((start > mid) & (start < mid_later), start, mid_later)
        seen = tuple(jnp.where(start <= top, start, old) for top, old in zip(tops, seen))
        return start + docs_ref[j], upper, later, mid_next, mid_later, seen

    zero = jnp.int32(0)
    far = jnp.int32(APART)
    _, upper, later, mid_next, mid_later, seen = lax.fori_loop(
        0, docs_ref.shape[0], doc, (zero, far, far, far, far, (zero,) * len(tops))
    )
    info_ref[INDEX] = index
    info_ref[BASE] = base
    info_ref[NEXT_START] = upper
    info_ref[LATER_START] = later
    info_ref[NEXT_BEGIN] = seen[-1]
    info_ref[MID_NEXT] = mid_next
    info_ref[MID_LATER] = mid_later
    info_ref[MID_BEGIN] = seen[-2]
    across = jnp.int32(tokens // 2)
    info_ref[MID_AHEAD] = jnp.where(upper >= mid, across, far)
    info_ref[MID_OWN] = jnp.where(later > mid, across, far)
    info_ref[MID_BACK] = jnp.where(mid_later > top, across, far)
    for j, ((begin, end), last) in enumerate(zip(spans, seen)):
        forward = j < len(ahead)
        joined = last < begin if forward else last <= end
        info_ref[FADES + j] = jnp.where(joined, end - begin if forward else begin - end, far)


def mask_kernel(docs_ref, dist_ref, begin_ref):
    tokens, lanes = begin_ref.shape
    base = lax.axis_index("ctx").astype(jnp.int32) * tokens
    row = column(tokens, lanes)
    begin_ref[...] = jnp.zeros_like(begin_ref)

    def doc(j, start):
        @pl.when((start > base) & (start < base + tokens))
        def _():
            begin_ref[...] = jnp.where(row >= start - base, start - base, begin_ref[...])

        return start + docs_ref[j]

    lax.fori_loop(0, docs_ref.shape[0], doc, jnp.int32(0))
    side = tokens // 2
    across = jnp.where(row >= side, side, 0)
    for low in range(0, side, lanes):
        spots = across + low + lax.broadcasted_iota(jnp.int32, (tokens, lanes), 1)
        allowed = (spots <= row) & (spots >= begin_ref[...])
        dist_ref[:, low : low + lanes] = jnp.where(allowed, (row - spots).astype(F32), F32(FAR))


def fade(rate, distance, shape):
    return jnp.exp(jnp.full(shape, -rate * distance.astype(F32), F32))


def spread(factor, block):
    return (block.reshape(-1, *factor.shape) * factor[None]).reshape(block.shape)


TILE = (8, 128)


def chip_kernel(at, base, info_ref, rate_ref, keep_ref, came_ref, keep_part_ref, send_part_ref):
    heads, quarter, _ = keep_part_ref.shape
    side = (info_ref[INDEX] >> 1) & 1
    for h in range(heads):
        rate = rate_ref[base + h]
        mine = fade(rate, info_ref[at], TILE)
        theirs = fade(rate, info_ref[at + 1], TILE)
        chip = spread(mine, keep_ref[h]) + spread(theirs, came_ref[h])
        low, high = chip[:quarter], chip[quarter:]
        keep_part_ref[h] = jnp.where(side == 0, low, high)
        send_part_ref[h] = jnp.where(side == 0, high, low)


def plane_kernel(at, base, info_ref, rate_ref, keep_ref, came_ref, out_ref):
    for h in range(out_ref.shape[0]):
        rate = rate_ref[base + h]
        mine = fade(rate, info_ref[at + 2], TILE)
        theirs = fade(rate, info_ref[at + 3], TILE)
        out_ref[h] = spread(mine, keep_ref[h]) + spread(theirs, came_ref[h])


def part_kernel(at, base, hops, first_side, info_ref, rate_ref, keep_ref, came_ref, *refs):
    moved, (own_ref, send_ref) = refs[:hops], refs[hops:]
    is_first = ((info_ref[INDEX] >> 1) & 1) == first_side
    for h in range(own_ref.shape[0]):
        rate = rate_ref[base + h]
        total = moved[0][h]
        for hop in range(1, hops):
            total += spread(fade(rate, info_ref[at + 5 + hop], TILE), moved[hop][h])
        earlier = jnp.where(is_first, keep_ref[h], came_ref[h])
        later = spread(fade(rate, info_ref[at + 4], TILE), total) + earlier
        own_ref[h] = jnp.where(is_first, total, later)
        send_ref[h] = jnp.where(is_first, later, total)


def half_kernel(at, base, first_core, info_ref, rate_ref, keep_ref, came_ref, own_ref, came_part_ref, mine_ref, send_ref):
    heads = own_ref.shape[0]
    index = info_ref[INDEX]
    is_first = (index & 1) == first_core
    low_side = ((index >> 1) & 1) == 0
    for h in range(heads):
        own, came = own_ref[h], came_part_ref[h]
        half = jnp.concatenate(
            [jnp.where(low_side, own, came), jnp.where(low_side, came, own)], axis=0
        )
        earlier = jnp.where(is_first, keep_ref[h], came_ref[h])
        later = spread(fade(rate_ref[base + h], info_ref[at + 5], TILE), half) + earlier
        mine_ref[h] = jnp.where(is_first, half, later).astype(BF16)
        send_ref[h] = jnp.where(is_first, later, half)


def by_side(row, first, second):
    return jnp.where(row < row.shape[0] // 2, first, second)


def state_kernel(docs_ref, rate_ref, k_ref, v_ref, kh_ref, vh_ref, send_ref, keep_ref, half_ref):
    tokens, heads, dim = k_ref.shape
    side = tokens // 2
    first = pl.program_id(0) * heads
    index = lax.axis_index("ctx")
    base = index * tokens
    mid, end = base + side, base + tokens

    def scan(j, carry):
        start, mid_last, last = carry
        mid_last = jnp.where(start <= mid - 1, start, mid_last)
        last = jnp.where(start <= end - 1, start, last)
        return (start + docs_ref[j], mid_last, last)

    _, mid_last, last = lax.fori_loop(0, docs_ref.shape[0], scan, (jnp.int32(0),) * 3)
    across = jnp.where(last < mid, jnp.int32(side), jnp.int32(APART))
    row = column(tokens, dim)
    distance = jnp.where(
        row + base >= by_side(row, mid_last, last),
        (by_side(row, side, tokens) - 1 - row).astype(F32),
        F32(FAR),
    )
    turned_k = jnp.swapaxes(k_ref[...], 0, 1)
    turned_v = jnp.swapaxes(v_ref[...], 0, 1)
    kh_ref[pl.ds(first, heads)] = turned_k
    vh_ref[pl.ds(first, heads)] = turned_v
    core = index & 1
    for h in range(heads):
        rate = rate_ref[first + h]
        tail = jnp.exp(-rate * distance)
        faded = (turned_k[h].astype(F32) * tail).astype(BF16)
        near = dot(faded[:side], turned_v[h, :side], TN)
        half_ref[first + h] = near
        state = spread(fade(rate, across, TILE), near) + dot(faded[side:], turned_v[h, side:], TN)
        split_halves(core, state, send_ref, keep_ref, first + h)


def turn_kernel(q_ref, g_ref, qh_ref, gh_ref):
    heads = q_ref.shape[1]
    here = pl.ds(pl.program_id(0) * heads, heads)
    qh_ref[here] = jnp.swapaxes(q_ref[...], 0, 1)
    gh_ref[here] = jnp.swapaxes(g_ref[...], 0, 1)


def scores_kernel(first, rows, rate_ref, qh_ref, kh_ref, vh_ref, dist_ref, out_ref, probs_ref):
    heads, tokens, _ = out_ref.shape

    def head(h, carry):
        full = first + h
        rate = rate_ref[full]
        for low in range(0, tokens, rows):
            here = slice(low, low + rows)
            scores = dot(qh_ref[full, here, :], kh_ref[full, here, :], NT)
            probs = (scores * jnp.exp(-rate * dist_ref[here, :])).astype(BF16)
            probs_ref[h, here, :] = probs
            out_ref[h, here, :] = dot(probs, vh_ref[full, here, :], NN).astype(BF16)
        return carry

    lax.fori_loop(0, heads, head, 0, unroll=2 if heads % 2 == 0 else 1)


def entry_distance(info_ref, row):
    side = row.shape[0] // 2
    return jnp.where(
        row + info_ref[BASE] < by_side(row, info_ref[NEXT_START], info_ref[MID_NEXT]),
        (row + 1 - by_side(row, 0, side)).astype(F32),
        F32(FAR),
    )


def reach_kernel(info_ref, rate_ref, qh_ref, gh_ref, gain_ref, far_ref, gained_ref):
    heads, tokens, dim = qh_ref.shape
    distance = entry_distance(info_ref, column(tokens, dim))
    for h in range(heads):
        far_ref[h] = (qh_ref[h].astype(F32) * jnp.exp(-rate_ref[h] * distance)).astype(BF16)
        gained_ref[h] = gain_ref[h : h + 1, :] * gh_ref[h].astype(F32)


def attend_kernel(groups, info_ref, rate_ref, far_ref, gained_ref, mine_ref, other_ref, half_ref, *refs):
    local_refs, (attn_ref, state_ref, mid_ref, stats_ref) = refs[:groups], refs[groups:]
    heads, tokens, dim = attn_ref.shape
    side = tokens // 2
    count = heads // groups
    core = info_ref[INDEX] & 1
    squares = jnp.zeros((tokens, dim), F32)
    cross = jnp.zeros((tokens, dim), F32)
    for h in range(heads):
        rate = rate_ref[h]
        put_halves(core, state_ref, h, mine_ref[h], other_ref[h])
        state = state_ref[h]
        mid = (spread(fade(rate, info_ref[MID_AHEAD], TILE), state.astype(F32)) + half_ref[h]).astype(BF16)
        mid_ref[h] = mid
        far = jnp.concatenate(
            [dot(far_ref[h, :side, :], state, NN), dot(far_ref[h, side:, :], mid, NN)], axis=0
        )
        near = local_refs[h // count][h % count].astype(F32)
        attn = near + far
        attn_ref[h] = attn.astype(BF16)
        squares += attn * attn
        cross += gained_ref[h] * attn
    stats_ref[0:1, :] = jnp.sum(jnp.swapaxes(squares, 0, 1), axis=0, keepdims=True)
    stats_ref[1:2, :] = jnp.sum(jnp.swapaxes(cross, 0, 1), axis=0, keepdims=True)


def lead_kernel(info_ref, rate_ref, qh_ref, faded_ref):
    heads, tokens, dim = qh_ref.shape
    row = column(tokens, dim)
    side = tokens // 2
    distance = jnp.where(
        row + info_ref[BASE] < by_side(row, info_ref[LATER_START], info_ref[MID_LATER]),
        (row - by_side(row, 0, side)).astype(F32),
        F32(FAR),
    )
    for h in range(heads):
        faded_ref[h] = (qh_ref[h].astype(F32) * jnp.exp(-rate_ref[h] * distance)).astype(BF16)


def norm_kernel(base, width, parts, info_ref, rate_ref, *refs):
    stats_refs, refs = refs[:parts], refs[parts:]
    attn_ref, gained_ref, faded_ref, grad_ref, send_ref, keep_ref, half_ref = refs
    heads, tokens, dim = grad_ref.shape
    core = info_ref[INDEX] & 1
    stats = stats_refs[0][...]
    for ref in stats_refs[1:]:
        stats = stats + ref[...]
    squares, cross = stats[0:1, :], stats[1:2, :]
    inverse = 1.0 / jnp.sqrt(squares / width + EPSILON)
    scale = cross * inverse * inverse * inverse / width
    inverse = jnp.swapaxes(jnp.broadcast_to(inverse, (dim, tokens)), 0, 1)
    scale = jnp.swapaxes(jnp.broadcast_to(scale, (dim, tokens)), 0, 1)
    side = tokens // 2
    for h in range(heads):
        full = base + h
        grad = (gained_ref[full] * inverse - attn_ref[full].astype(F32) * scale).astype(BF16)
        grad_ref[h] = grad
        faded = faded_ref[full]
        near = dot(faded[side:], grad[side:], TN)
        half_ref[h] = near
        state = dot(faded[:side], grad[:side], TN)
        state += spread(fade(rate_ref[full], info_ref[MID_OWN], TILE), near)
        split_halves(core, state, send_ref, keep_ref, h)


def grads_kernel(base, first, rows, info_ref, rate_ref, grad_ref, qh_ref, kh_ref, vh_ref, probs_ref, dist_ref, state_ref, mid_ref, dq_ref, dk_ref, dv_ref):
    heads, tokens, dim = dq_ref.shape
    distance = entry_distance(info_ref, column(tokens, dim))

    def head(h, carry):
        near = first + h
        full = base + near
        rate = rate_ref[full]
        factor = jnp.exp(-rate * distance)
        for low, entry_ref in ((0, state_ref), (rows, mid_ref)):
            here = slice(low, low + rows)
            grad = grad_ref[near, here, :]
            raw = dot(grad, vh_ref[full, here, :], NT)
            weights = (raw * jnp.exp(-rate * dist_ref[here, :])).astype(BF16)
            dq = dot(weights, kh_ref[full, here, :], NN)
            dq += factor[here] * dot(grad, entry_ref[full], NT)
            dq_ref[h, here, :] = dq.astype(BF16)
            dk_ref[h, here, :] = dot(weights, qh_ref[full, here, :], TN).astype(BF16)
            dv_ref[h, here, :] = dot(probs_ref[h, here, :], grad, TN).astype(BF16)
        return carry

    lax.fori_loop(0, heads, head, 0, unroll=2 if heads % 2 == 0 else 1)


def turn_back_kernel(steps, *refs):
    parts, out_ref = refs[:-1], refs[-1]
    each = len(parts) // steps
    for s in range(steps):

        @pl.when(pl.program_id(0) == s)
        def _():
            block = [ref[...] for ref in parts[s * each : (s + 1) * each]]
            out_ref[...] = jnp.swapaxes(jnp.concatenate(block, axis=0), 0, 1)


def return_kernel(info_ref, rate_ref, kh_ref, vh_ref, far_k_ref, far_v_ref):
    heads, tokens, dim = kh_ref.shape
    row = column(tokens, dim)
    distance = jnp.where(
        row + info_ref[BASE] >= by_side(row, info_ref[MID_BEGIN], info_ref[NEXT_BEGIN]),
        (by_side(row, tokens // 2, tokens) - row).astype(F32),
        F32(FAR),
    )
    for h in range(heads):
        factor = jnp.exp(-rate_ref[h] * distance)
        far_k_ref[h] = (kh_ref[h].astype(F32) * factor).astype(BF16)
        far_v_ref[h] = (vh_ref[h].astype(F32) * factor).astype(BF16)


def finish_kernel(base, groups, info_ref, rate_ref, far_k_ref, far_v_ref, mine_ref, other_ref, half_ref, *refs):
    dk_parts, dv_parts = refs[:groups], refs[groups : 2 * groups]
    dk_ref, dv_ref, state_ref = refs[-3:]
    heads = mine_ref.shape[0]
    count, tokens, _ = dk_parts[0].shape
    side = tokens // 2
    core = info_ref[INDEX] & 1

    def block(low):
        here = slice(low, low + side)
        dks, dvs = [], []
        for h in range(heads):
            full = base + h
            if low == 0:
                put_halves(core, state_ref, h, mine_ref[h], other_ref[h])
            state = state_ref[h]
            if low == 0:
                faded = spread(fade(rate_ref[full], info_ref[MID_BACK], TILE), state.astype(F32))
                state = (faded + half_ref[h]).astype(BF16)
            dk = dk_parts[h // count][h % count, here, :].astype(F32)
            dv = dv_parts[h // count][h % count, here, :].astype(F32)
            dk += dot(far_v_ref[full, here, :], state, NT)
            dv += dot(far_k_ref[full, here, :], state, NN)
            dks.append(dk.astype(BF16))
            dvs.append(dv.astype(BF16))
        dk_ref[...] = jnp.swapaxes(jnp.stack(dks), 0, 1)
        dv_ref[...] = jnp.swapaxes(jnp.stack(dvs), 0, 1)

    for s in range(2):
        pl.when(pl.program_id(0) == s)(partial(block, s * side))


def send(block, axis, target):
    count = lax.axis_size(axis)
    route = [(i, target(i)) for i in range(count) if 0 <= target(i) < count]
    return lax.ppermute(block, axis, route)


def hop_count(tokens):
    return -(-LONGEST // (4 * tokens))


def entering_state(leave, keep, info, rates, base, forward, hops):
    heads, rows, dim = keep.shape
    at = FADES + (0 if forward else len(fade_rows(hops)[0]))
    first = 0 if forward else 1
    step = 4 if forward else -4
    part = jax.ShapeDtypeStruct((heads, rows // 2, dim), F32)
    half = jax.ShapeDtypeStruct(keep.shape, F32)

    def combine(kernel, arrays, outs):
        return run(
            kernel,
            [info, rates, *arrays],
            [SMEM, SMEM] + [VMEM] * len(arrays),
            outs,
            [VMEM] * len(outs),
            cost=(0, 4 * heads * rows * dim),
        )

    came_half = send(leave, "ctx", lambda i: i ^ 1)
    keep_part, send_part = combine(partial(chip_kernel, at, base), [keep, came_half], [part] * 2)
    came_part = send(send_part, "ctx", lambda i: i ^ 2)
    (moving,) = combine(partial(plane_kernel, at, base), [keep_part, came_part], [part])
    moved = []
    for _ in range(hops):
        moving = send(moving, "ctx", lambda i: i + step)
        moved.append(moving)
    own, send_part = combine(
        partial(part_kernel, at, base, hops, first), [keep_part, came_part, *moved], [part] * 2
    )
    came = send(send_part, "ctx", lambda i: i ^ 2)
    mine, send_half = combine(
        partial(half_kernel, at, base, first),
        [keep, came_half, own, came],
        [jax.ShapeDtypeStruct(keep.shape, BF16), half],
    )
    return mine, send(send_half, "ctx", lambda i: i ^ 1)


def head_sum_parts(stats):
    count = lax.axis_size("head")
    if count & (count - 1):
        return [stats] + [
            lax.ppermute(stats, "head", [(i, (i + d) % count) for i in range(count)])
            for d in range(1, count)
        ]
    parts, bit = [stats], 1
    while bit < count:
        stats = parts[0] if len(parts) == 1 else parts[0] + parts[1]
        parts = [stats, send(stats, "head", lambda i: i ^ bit)]
        bit *= 2
    return parts


SMEM = pl.BlockSpec(memory_space=pltpu.SMEM)
VMEM = pl.BlockSpec(memory_space=pltpu.VMEM)


def kept(*arrays):
    return [pltpu.with_memory_space_constraint(a, pltpu.VMEM) for a in arrays]


def at_hand(*arrays):
    return [pltpu.with_memory_space_constraint(a, pltpu.SMEM) for a in arrays]


def streamed(*arrays):
    return [pltpu.with_memory_space_constraint(a, pltpu.HBM) for a in arrays]


def run(kernel, args, specs, outs, out_specs, steps=None, scratch=(), alias=None, cost=(0, 0)):
    return pl.pallas_call(
        kernel,
        out_shape=outs,
        grid=() if steps is None else (steps,),
        in_specs=specs,
        out_specs=out_specs,
        scratch_shapes=scratch,
        input_output_aliases=alias or {},
        cost_estimate=pl.CostEstimate(flops=cost[0], bytes_accessed=cost[1], transcendentals=0),
        compiler_params=pltpu.CompilerParams(vmem_limit_bytes=16 << 20),
    )(*args)


def body(queries, keys, values, out_grad, gain, rates, docs):
    tokens, heads, dim = queries.shape
    wide = 8 if heads % 8 == 0 else heads
    count = 2 if wide % 2 == 0 else wide
    span = wide
    steps, groups = heads // wide, span // count
    total_groups = heads // count
    rows = tokens // 2
    hops = hop_count(tokens)
    width = heads * dim * lax.axis_size("head")
    chunks = range(heads // span)
    shape = lambda *s: jax.ShapeDtypeStruct(s, F32)
    major = pltpu.VMEM((heads, tokens, dim), BF16)
    chunk = pltpu.VMEM((span, tokens, dim), BF16)
    some = pltpu.VMEM((count, tokens, dim), BF16)
    half = shape(span, dim // 2, dim)
    token_block = pl.BlockSpec((tokens, wide, dim), lambda i: (0, i, 0))
    unit = heads * tokens * dim
    rates, docs, gain = streamed(rates, docs, gain)

    kh, vh, leave, keep, early = run(
        state_kernel,
        [docs, rates, *streamed(keys, values)],
        [SMEM, SMEM, token_block, token_block],
        [major, major] + [shape(heads, dim // 2, dim)] * 2 + [pltpu.VMEM((heads, dim, dim), F32)],
        [VMEM] * 5,
        steps=steps,
        cost=(2 * unit * dim, 8 * unit),
    )

    spans = sum(len(rows) for rows in fade_rows(hops))
    info, rates = run(
        partial(setup_kernel, hops, tokens),
        [docs, rates],
        [SMEM] * 2,
        [pltpu.SMEM((FADES + spans,), jnp.int32), pltpu.SMEM((heads,), F32)],
        [SMEM] * 2,
    )
    info, rates = at_hand(info, rates)
    distance = run(
        mask_kernel,
        [docs],
        [SMEM],
        pltpu.VMEM((tokens, rows), F32),
        VMEM,
        scratch=[pltpu.VMEM((tokens, dim), jnp.int32)],
        cost=(0, 2 * tokens * tokens),
    )

    qh, gh = run(
        turn_kernel,
        streamed(queries, out_grad),
        [token_block, token_block],
        [major, major],
        [VMEM, VMEM],
        steps=steps,
        cost=(0, 8 * unit),
    )
    near, probs = [], []
    for g in range(total_groups):
        n, p = run(
            partial(scores_kernel, g * count, rows),
            [rates, *kept(qh, kh, vh, distance)],
            [SMEM] + [VMEM] * 4,
            [some, pltpu.VMEM((count, tokens, rows), BF16)],
            [VMEM] * 2,
            cost=(4 * unit * tokens // total_groups, 0),
        )
        near.append(n), probs.append(p)

    far, gained = run(
        reach_kernel,
        [info, rates, *kept(qh, gh), gain],
        [SMEM, SMEM] + [VMEM] * 3,
        [major, pltpu.VMEM((heads, tokens, dim), F32)],
        [VMEM] * 2,
        cost=(4 * unit, 0),
    )

    mine, other = entering_state(leave, keep, info, rates, 0, True, hops)
    states = pltpu.VMEM((heads, dim, dim), BF16)
    attn, states, mids, stats = run(
        partial(attend_kernel, total_groups),
        [info, rates, *kept(far, gained), mine, other, *kept(early, *near)],
        [SMEM, SMEM] + [VMEM] * (5 + total_groups),
        [major, states, states, shape(2, tokens)],
        [VMEM] * 4,
        cost=(2 * unit * dim, 0),
    )
    parts = head_sum_parts(stats)

    faded = run(
        lead_kernel, [info, rates, *kept(qh)], [SMEM, SMEM, VMEM], major, VMEM, cost=(2 * unit, 0)
    )
    grads, halves, late = [], [], []
    for c in chunks:
        g, *pair, n = run(
            partial(norm_kernel, c * span, width, len(parts)),
            [info, rates, *parts, *kept(attn, gained, faded)],
            [SMEM, SMEM] + [VMEM] * (len(parts) + 3),
            [chunk, half, half, pltpu.VMEM((span, dim, dim), F32)],
            [VMEM] * 4,
            cost=(2 * unit * dim // len(chunks), 0),
        )
        grads.append(g), halves.extend(pair), late.append(n)

    dqh, dk_part, dv_part = [], [], []
    for g in range(total_groups):
        c, at = divmod(g, groups)
        parts = run(
            partial(grads_kernel, c * span, at * count, rows),
            [info, rates, *kept(grads[c], qh, kh, vh, probs[g], distance, states, mids)],
            [SMEM, SMEM] + [VMEM] * 8,
            [some] * 3,
            [VMEM] * 3,
            cost=(8 * unit * tokens // total_groups, 0),
        )
        for kind, part in zip((dqh, dk_part, dv_part), parts):
            kind.append(part)
    full = jax.ShapeDtypeStruct((tokens, heads, dim), BF16)
    dq = run(
        partial(turn_back_kernel, steps),
        kept(*dqh),
        [VMEM] * total_groups,
        full,
        token_block,
        steps=steps,
        cost=(0, 2 * unit),
    )

    far_k, far_v = run(
        return_kernel,
        [info, rates, *kept(kh, vh)],
        [SMEM, SMEM] + [VMEM] * 2,
        [major] * 2,
        [VMEM] * 2,
        cost=(4 * unit, 0),
    )
    entered = [
        entering_state(*halves[2 * c : 2 * c + 2], info, rates, c * span, False, hops)
        for c in chunks
    ]
    made = []
    for c in chunks:
        mine, other = entered[c]
        here = slice(c * groups, (c + 1) * groups)
        args = [info, rates, *kept(far_k, far_v), mine, other, *kept(late[c], *dk_part[here], *dv_part[here])]
        specs = [SMEM, SMEM] + [VMEM] * (5 + 2 * groups)
        alias = {len(args) + j: j for j in range(len(made))}
        block = pl.BlockSpec((rows, wide, dim), lambda i, c=c: (i, c, 0))
        made = run(
            partial(finish_kernel, c * span, groups),
            args + list(made),
            specs + [pl.BlockSpec(memory_space=pl.ANY)] * len(made),
            [full, full],
            [block, block],
            steps=2,
            scratch=[pltpu.VMEM((wide, dim, dim), BF16)],
            alias=alias,
            cost=(4 * unit * dim // len(chunks), 4 * unit // len(chunks)),
        )
    return dq, *made


def solution(mesh):
    token, head = P("ctx", "head", None), P("head")
    return jax.shard_map(
        body,
        mesh=mesh,
        in_specs=(token, token, token, token, P("head", None), head, P()),
        out_specs=(token, token, token),
        check_vma=False,
    )
```
